32 devices in a mesh: grp: 2 (over y), freq: 4 (over z), panel: 4 (over x, core).
Axes of the slice: x: 2, y: 2, z: 4, core: 2. Of those that a mesh axis runs over, the one named last changes fastest.
Arguments:
- traces: float32 [1024, 3072], P('freq', ('grp', 'panel')), parts along dimension 1, may hold values from -6 to 6
- centroids: float32 [3, 3072], P(None, ('grp', 'panel')), parts along dimension 1, may hold values from -1 to 1
- near_list: int32 [8, 8, 2], P(('grp', 'panel')), parts along dimension 0, may hold values from 0 to 4, as said below
- pair_count: int32 [8], P(('grp', 'panel')), parts along dimension 0, may hold values from 5 to 8, as said below
Outputs:
- field: float32 [1024, 3072], P('freq', ('grp', 'panel')), parts along dimension 1
The draws below stay inside these ranges and needn't reach their ends.
There are 2 independent parts, one for each index of `grp`. The reference program is written for one: setup_inputs(seed, part) draws one part's arguments, and reference() takes and returns one part's arrays. A program takes and returns all parts, laid end to end along the dimension named above; each array names one. Nothing has to cross between parts.
Inputs may be any that keep to these rules, and one draw needn't show every extreme that they name: `near_list`: each row holds a row block below 3 and an extended column block up to 4; in every shard, pair n < 3 is (n, n + 1), pair 3 is (0, 0) and pair 4 is (2, 4); pairs may repeat; entries past the count are valid but unused. `pair_count`: some shard holds 8 pairs in every draw.
All inputs are finite; a program needn't handle non-finite values.
Results may differ from the reference program's by a relative error of at most 0.0003.
Values sent between devices are 32-bit elements; how exact they have to be, the bound alone decides.
A program may use at most 64 MiB of HBM per device.

```python
import math
import jax
import jax.numpy as jnp
from jax import lax

NT = 1024
BLK = 128
NB = 3
MAXP = 8
PD = 384
SHARDS = 4
NP = 1536
KH = 512
N_PANEL = 4


def pair_tables(key):
    base = jax.random.fold_in(key, 11)
    key_extra, key_top, key_rows, key_cols = jax.random.split(base, 4)
    extra = jax.random.randint(key_extra, (SHARDS,), 2, MAXP - NB + 1)
    chosen = jax.random.randint(key_top, (), 0, SHARDS)
    extra = jnp.where(jnp.arange(SHARDS) == chosen, MAXP - NB, extra)
    counts = (NB + extra).astype(jnp.int32)
    rows = jax.random.randint(key_rows, (SHARDS, MAXP), 0, NB)
    cols = jax.random.randint(key_cols, (SHARDS, MAXP), 0, NB + 2)
    slot = jnp.arange(MAXP)[None, :] + jnp.zeros((SHARDS, 1), jnp.int32)
    rows = jnp.where(slot < NB, slot, rows)
    cols = jnp.where(slot < NB, slot + 1, cols)
    rows = jnp.where(slot == NB, 0, rows)
    cols = jnp.where(slot == NB, 0, cols)
    rows = jnp.where(slot == NB + 1, NB - 1, rows)
    cols = jnp.where(slot == NB + 1, NB + 1, cols)
    return (jnp.stack([rows, cols], axis=-1).astype(jnp.int32), counts)


def draw_near_list(key, part):
    return pair_tables(key)[0]


def draw_pair_count(key, part):
    return pair_tables(key)[1]


def shard_levels(stream_key, extent, cuts, low, high):
    def one(dim, shards_of):
        draws = jax.random.uniform(jax.random.fold_in(jax.random.fold_in(stream_key, 6), dim), (shards_of,), jnp.float32, low / len(cuts), high / len(cuts))
        return jnp.repeat(jnp.exp(draws), extent[dim] // shards_of).reshape((-1,) + (1,) * (len(extent) - dim - 1))

    level = one(*cuts[0])
    for cut in cuts[1:]:
        level = level * one(*cut)
    return level


def noise(stream_key, shape, width, bound, cuts=(), kind=jnp.bfloat16):
    array = width * jax.random.normal(stream_key, shape, jnp.float32)
    if cuts:
        array = array * shard_levels(stream_key, shape, cuts, -0.22, 0.18)
    return jnp.clip(array, -bound, bound).astype(kind)


def setup_inputs(seed: int = 0, part: int = 0) -> dict:
    keys = jax.random.split(jax.random.key(seed), 5)
    own_keys = jax.random.split(jax.random.fold_in(keys[4], part), 5)
    return {
        "traces": noise(own_keys[0], (NT, NP), 1.0, 6.0, ((0, 4), (1, 4)), jnp.float32),
        "centroids": jnp.clip(jax.random.uniform(own_keys[1], (3, NP), jnp.float32, -1.0, 1.0) * shard_levels(own_keys[1], (3, NP), ((1, 4),), -0.4, 0.0), -1.0, 1.0),
        "near_list": draw_near_list(jax.random.fold_in(jax.random.fold_in(keys[4], part), 71), part),
        "pair_count": draw_pair_count(jax.random.fold_in(jax.random.fold_in(keys[4], part), 71), part),
    }


damping = 0.999
time_step = 0.5
core_square = 0.01
highest = lax.Precision.HIGHEST

def forward_tables(times, freqs):
    product = freqs[:, None] * times[None, :] % NT
    angle = 2.0 * math.pi / NT * product.astype(jnp.float32)
    decay = jnp.exp(times.astype(jnp.float32) * math.log(damping))
    return (jnp.cos(angle) * decay[None, :], -jnp.sin(angle) * decay[None, :])

def inverse_tables(times, freqs):
    product = times[:, None] * freqs[None, :] % NT
    angle = 2.0 * math.pi / NT * product.astype(jnp.float32)
    growth = jnp.exp(-times.astype(jnp.float32) * math.log(damping)) / NT
    weight = jnp.where(freqs == 0, 1.0, 2.0).astype(jnp.float32)
    scale = growth[:, None] * weight[None, :]
    return (jnp.cos(angle) * scale, jnp.sin(angle) * scale)

def laplace(freqs):
    angle = 2.0 * math.pi / NT * freqs.astype(jnp.float32)
    return ((1.0 - damping * jnp.cos(angle)) / time_step, damping * jnp.sin(angle) / time_step)

def block_kernel(rows_xyz, cols_xyz, lap_re, lap_im):
    diff = rows_xyz[:, :, None] - cols_xyz[:, None, :]
    dist = jnp.sqrt(lax.optimization_barrier(jnp.sum(diff * diff, axis=0)) + core_square)
    decay = jnp.exp(-lap_re[:, None, None] * dist[None]) / (4.0 * math.pi * dist[None])
    phase = lap_im[:, None, None] * dist[None]
    return (decay * jnp.cos(phase), -decay * jnp.sin(phase))

def apply_pairs(ext_re, ext_im, ext_xyz, shard_list, count, lap_re, lap_im):
    kcount = ext_re.shape[0]
    own = ext_re.shape[1] - 2 * BLK

    def add_pair(slot, acc):
        acc_re, acc_im = acc
        row = shard_list[slot, 0].astype(jnp.int32)
        col = shard_list[slot, 1].astype(jnp.int32)
        rows_xyz = lax.dynamic_slice_in_dim(ext_xyz, (row + 1) * BLK, BLK, 1)
        cols_xyz = lax.dynamic_slice_in_dim(ext_xyz, col * BLK, BLK, 1)
        g_re = lax.dynamic_slice_in_dim(ext_re, col * BLK, BLK, 1)
        g_im = lax.dynamic_slice_in_dim(ext_im, col * BLK, BLK, 1)
        k_re, k_im = block_kernel(rows_xyz, cols_xyz, lap_re, lap_im)
        new_re = jnp.einsum('kij,kj->ki', k_re, g_re, precision=highest) - jnp.einsum('kij,kj->ki', k_im, g_im, precision=highest)
        new_im = jnp.einsum('kij,kj->ki', k_re, g_im, precision=highest) + jnp.einsum('kij,kj->ki', k_im, g_re, precision=highest)
        start = row * BLK
        acc_re = lax.dynamic_update_slice_in_dim(acc_re, lax.dynamic_slice_in_dim(acc_re, start, BLK, 1) + new_re, start, 1)
        acc_im = lax.dynamic_update_slice_in_dim(acc_im, lax.dynamic_slice_in_dim(acc_im, start, BLK, 1) + new_im, start, 1)
        return (acc_re, acc_im)
    zeros = jnp.zeros((kcount, own), jnp.float32)
    return lax.fori_loop(jnp.int32(0), count.astype(jnp.int32), add_pair, (zeros, zeros))

def reference(traces, centroids, near_list, pair_count):
    times = jnp.arange(NT, dtype=jnp.int32)
    freqs = jnp.arange(KH, dtype=jnp.int32)
    fcos, fsin = forward_tables(times, freqs)
    spec_re = jnp.dot(fcos, traces, precision=highest)
    spec_im = jnp.dot(fsin, traces, precision=highest)
    lap_re, lap_im = laplace(freqs)
    ext_index = (jnp.arange(N_PANEL, dtype=jnp.int32)[:, None] * PD - BLK + jnp.arange(PD + 2 * BLK, dtype=jnp.int32)[None, :]) % NP

    def shard_apply(shard):
        cols = ext_index[shard]
        return apply_pairs(spec_re[:, cols], spec_im[:, cols], centroids[:, cols], near_list[shard], pair_count[shard], lap_re, lap_im)
    out_re, out_im = lax.map(shard_apply, jnp.arange(N_PANEL, dtype=jnp.int32))
    out_re = jnp.transpose(out_re, (1, 0, 2)).reshape(KH, NP)
    out_im = jnp.transpose(out_im, (1, 0, 2)).reshape(KH, NP)
    icos, isin = inverse_tables(times, freqs)
    return jnp.dot(icos, out_re, precision=highest) - jnp.dot(isin, out_im, precision=highest)
```

```python
import math

import jax
import jax.numpy as jnp
from jax import lax
from jax.experimental import pallas as pl
from jax.experimental.pallas import tpu as pltpu
from jax.sharding import PartitionSpec as P

NT = 1024
BLK = 128
GEO = 8
TAIL = 24
HEAD = 32
PAD = 8
START = PAD + HEAD
LEAD = 16
HALF = 12
CORR = 8
FIXED = 5
WIDE = 2 * BLK

SCALE = 512.0
FIELD_UP = 32.0
LOW_UP = 8192.0
TERM_UP = 256.0

damping = 0.999
time_step = 0.5
core_square = 0.01

bf16 = jnp.bfloat16
fp8 = jnp.float8_e4m3fn
f32 = jnp.float32


def product(x, y):
    return jnp.dot(x, y, preferred_element_type=f32)


def split(v):
    hi = v.astype(bf16)
    return hi, v - hi.astype(f32)


def turn(geometry):
    return jnp.concatenate([geometry] * (BLK // GEO), axis=0).T


def spread(ext, pair_data, four_data, c, first, rows):
    for n in range(4):
        v = ext[c, PAD + first - n : PAD + first - n + rows, :]
        hi, low = split(v)
        if n < 2:
            pair_data[c, first : first + rows, n * BLK : (n + 1) * BLK] = hi
        four_data[c, first : first + rows, n * BLK : (n + 1) * BLK] = (v * FIELD_UP).astype(fp8)
        four_data[c, first : first + rows, (4 + n) * BLK : (5 + n) * BLK] = (low * LOW_UP).astype(fp8)


def fill(main, fine, sample, p, theirs, mine):
    square = jnp.full((BLK, BLK), core_square, f32)
    for a in range(3):
        diff = theirs[:, a : a + 1] - mine[a : a + 1, :]
        square = square + diff * diff
    dist = jnp.sqrt(square)
    x = dist * (1.0 / time_step)
    term = jnp.exp(-x) * (SCALE / (4.0 * math.pi)) / dist
    hi, low = split(term * jnp.exp(-damping * x))
    sample[p, :, :BLK] = hi
    sample[p, :, BLK:] = low.astype(bf16)
    for n in range(TAIL):
        side, place = divmod(n, HALF)
        hi, low = split(term)
        main[p, place * BLK : (place + 1) * BLK, side * BLK : (side + 1) * BLK] = hi
        if n < 2 * CORR:
            side, place = divmod(n, CORR)
            first = (place // 4 * 8 + place % 4) * BLK
            lanes = slice(side * BLK, (side + 1) * BLK)
            fine[p, first : first + BLK, lanes] = (low * TERM_UP).astype(fp8)
            fine[p, first + 4 * BLK : first + 5 * BLK, lanes] = term.astype(fp8)
        if n + 1 < TAIL:
            term = term * (x * (1.0 / (n + 1)))


def contract(pair_data, four_data, main, fine, wide, narrow, p, c, first, last):
    rows = last - first
    total = None
    for k in range(HALF // 2):
        start = HEAD - LEAD + first - 2 * k
        term = product(pair_data[c, start : start + rows, :], main[p, k * WIDE : (k + 1) * WIDE, :])
        total = term if total is None else total + term
    wide[p, first:last, :] = total
    total = None
    for k in range(CORR // 4):
        start = HEAD - LEAD + first - 4 * k
        term = product(four_data[c, start : start + rows, :], fine[p, k * 8 * BLK : (k + 1) * 8 * BLK, :])
        total = term if total is None else total + term
    narrow[p, first:last, :] = total


def gather(wide, narrow, p, first, last):
    a, b = LEAD + first, LEAD + last
    low = narrow[p, a:b, :BLK] + narrow[p, a - CORR : b - CORR, BLK:]
    high = wide[p, a:b, :BLK] + wide[p, a - HALF : b - HALF, BLK:]
    return high + low * (1.0 / (FIELD_UP * TERM_UP))


def operator(
    list_hbm,
    count_hbm,
    traces_ref,
    xyz_hbm,
    out_ref,
    ext,
    head,
    slots,
    xyz_ref,
    list_ref,
    count_ref,
    pair_data,
    four_data,
    main,
    fine,
    sample,
    wide,
    narrow,
    turned,
    shape,
    send,
    recv,
    load,
):
    steps, width = traces_ref.shape
    blocks = width // BLK
    geo = START + steps
    groups = lax.axis_size("freq")
    shards = lax.axis_size("panel")
    position = lax.axis_index("freq")
    shard = lax.axis_index("panel")
    pairs = list_ref.shape[1]
    rows = steps + LEAD

    def device(ahead, side):
        return {
            "freq": lax.rem(position + ahead + groups, groups),
            "panel": lax.rem(shard + side + shards, shards),
        }

    def remote(i, ahead, side, source, target):
        return pltpu.make_async_remote_copy(
            src_ref=source,
            dst_ref=target,
            send_sem=send.at[i],
            recv_sem=recv.at[i],
            device_id=device(ahead, side),
            device_id_type=pl.DeviceIdType.MESH,
        )

    peers = [(0, 1), (0, -1)] + [(s, 0) for s in range(1, groups)]
    barrier = pltpu.get_barrier_semaphore()
    for s, d in peers:
        pl.semaphore_signal(
            barrier, inc=1, device_id=device(s, d), device_id_type=pl.DeviceIdType.MESH
        )
    loads = [
        pltpu.make_async_copy(
            traces_ref.at[:, pl.ds(b * BLK, BLK)],
            ext.at[b + 1, pl.ds(START, steps)],
            load.at[b],
        )
        for b in range(blocks)
    ]
    loads.append(pltpu.make_async_copy(xyz_hbm, xyz_ref, load.at[blocks]))
    loads.append(pltpu.make_async_copy(list_hbm, list_ref, load.at[blocks + 1]))
    loads.append(pltpu.make_async_copy(count_hbm, count_ref, load.at[blocks + 2]))
    for copy in loads:
        copy.start()

    rest = pl.ds(START, steps - TAIL)
    tail = pl.ds(START + steps - TAIL, TAIL)
    lanes = (pl.ds((blocks - 1) * BLK, BLK), pl.ds(0, BLK))
    early, place = pl.ds(0, steps - TAIL), pl.ds(steps - TAIL, TAIL)
    ends = [
        remote(0, 0, 1, traces_ref.at[place, lanes[0]], ext.at[0, tail]),
        remote(1, 0, -1, traces_ref.at[place, lanes[1]], ext.at[blocks + 1, tail]),
    ]
    edges = [
        remote(2, 0, 1, traces_ref.at[early, lanes[0]], ext.at[0, rest]),
        remote(3, 0, -1, traces_ref.at[early, lanes[1]], ext.at[blocks + 1, rest]),
    ]
    spot = pl.ds(geo, GEO)
    marks = [
        remote(4, 0, 1, ext.at[blocks, spot], ext.at[0, spot]),
        remote(5, 0, -1, ext.at[1, spot], ext.at[blocks + 1, spot]),
    ]
    every = pl.ds(0, blocks + 2)
    turns = [remote(6, 1, 0, ext.at[every, pl.ds(geo - TAIL, TAIL + GEO)], head)]
    for s in range(2, groups):
        turns.append(remote(5 + s, s, 0, ext.at[every, spot], slots.at[s]))

    pl.semaphore_wait(barrier, len(peers))
    for copy in ends + edges:
        copy.start()

    times = position * steps + lax.broadcasted_iota(jnp.int32, (steps, BLK), 0)
    weight = jnp.exp(times.astype(f32) * math.log(damping))
    weight = jnp.where(times % 2 == 0, weight, -weight)
    for copy in loads[blocks:]:
        copy.wait()
    for b in range(blocks):
        loads[b].wait()
        own = ext[b + 1, START:geo, :]
        part = jnp.sum(weight * own, axis=0, keepdims=True)
        ext[b + 1, geo : geo + 3, :] = xyz_ref[:, b * BLK : (b + 1) * BLK]
        ext[b + 1, geo + 3 : geo + 4, :] = part
        ext[b + 1, geo + 4 : geo + GEO, :] = jnp.zeros((GEO - 4, BLK), f32)
    for copy in marks:
        copy.start()

    ext[:, :START, :] = jnp.zeros((blocks + 2, START, BLK), f32)
    for c in range(1, blocks + 1):
        spread(ext, pair_data, four_data, c, HEAD, steps)
        shape[c] = ext[c, geo : geo + GEO, :]
        turned[c] = turn(shape[c])
    fixed = [(n, n + 1) for n in range(blocks)] + [(0, 0), (blocks - 1, blocks + 1)]
    for p, (r, c) in enumerate(fixed[:blocks]):
        fill(main, fine, sample, p, turned[c], shape[r + 1])
        contract(pair_data, four_data, main, fine, wide, narrow, p, c, HEAD, rows)

    for copy in ends + marks:
        copy.wait()
    for copy in turns:
        copy.start()
    for c in (0, blocks + 1):
        shape[c] = ext[c, geo : geo + GEO, :]
        turned[c] = turn(shape[c])
    order = [(jnp.int32(r), jnp.int32(c)) for r, c in fixed]
    order += [(list_ref[0, p], list_ref[1, p]) for p in range(len(fixed), pairs)]
    for p in range(blocks, pairs):
        r, c = order[p] if p >= len(fixed) else fixed[p]
        fill(main, fine, sample, p, turned[c], shape[r + 1])

    for copy in edges:
        copy.wait()
    for c in (0, blocks + 1):
        spread(ext, pair_data, four_data, c, HEAD + LEAD, steps - LEAD)
    turns[0].wait()
    around = jnp.where(position == 0, math.exp(NT * math.log(damping)), 1.0)
    for c in range(blocks + 2):
        ext[c, START - TAIL : START, :] = head[c, :TAIL, :] * around
    for c in range(blocks + 2):
        spread(ext, pair_data, four_data, c, 0, HEAD + LEAD)
    for p in range(blocks):
        r, c = fixed[p]
        contract(pair_data, four_data, main, fine, wide, narrow, p, c, 0, HEAD)
    for p in range(blocks, pairs):
        r, c = order[p] if p >= len(fixed) else fixed[p]
        contract(pair_data, four_data, main, fine, wide, narrow, p, c, 0, rows)

    for copy in turns[1:]:
        copy.wait()
    sides = []
    pick = lax.broadcasted_iota(jnp.int32, (2 * GEO, BLK), 0)
    for c in range(blocks + 2):
        total = ext[c, geo + 3 : geo + 4, :] + head[c, TAIL + 3 : TAIL + 4, :]
        for s in range(2, groups):
            total = total + slots[s, c, 3:4, :]
        hi, low = split(total)
        turned[c, : 2 * GEO, :] = jnp.where(pick == 0, total, jnp.where(pick == 1, low, 0.0))
    local = lax.broadcasted_iota(jnp.int32, (steps, BLK), 0)
    growth = jnp.exp((position * steps + local).astype(f32) * -math.log(damping)) / NT
    growth = jnp.where(local % 2 == 0, -growth, growth)

    def whole(p, c):
        both = product(turned[c, : 2 * GEO, :].astype(bf16), sample[p])
        sums = both[0:1, :BLK] + (both[1:2, :BLK] + both[0:1, BLK:])
        return gather(wide, narrow, p, 0, steps) + growth * sums

    for r in range(blocks):
        total = whole(r, r + 1)
        for p in range(blocks, len(fixed)):
            if fixed[p][0] == r:
                total = total + whole(p, fixed[p][1])
        out_ref[:, r * BLK : (r + 1) * BLK] = total
    for p in range(len(fixed), pairs):
        total = whole(p, order[p][1])
        target = jnp.where(p < count_ref[0], order[p][0], blocks)
        for r in range(blocks):
            lanes = slice(r * BLK, (r + 1) * BLK)
            out_ref[:, lanes] = out_ref[:, lanes] + jnp.where(target == r, total, 0.0)
    out_ref[...] = out_ref[...] * (1.0 / SCALE)


def per_device(traces, centroids, near_list, pair_count):
    steps, width = traces.shape
    blocks = width // BLK
    pairs = near_list.shape[1]
    groups = lax.axis_size("freq")
    count = 5 + groups
    hbm = pl.BlockSpec(memory_space=pltpu.HBM)
    given = [pltpu.with_memory_space_constraint(v, pltpu.HBM) for v in (traces, centroids)]
    return pl.pallas_call(
        operator,
        out_shape=pltpu.VMEM((steps, width), f32),
        in_specs=[hbm] * 4,
        out_specs=pl.BlockSpec(memory_space=pltpu.VMEM),
        scratch_shapes=[
            pltpu.VMEM((blocks + 2, START + steps + GEO, BLK), f32),
            pltpu.VMEM((blocks + 2, TAIL + GEO, BLK), f32),
            pltpu.VMEM((groups, blocks + 2, GEO, BLK), f32),
            pltpu.VMEM((3, width), f32),
            pltpu.SMEM((2, pairs), jnp.int32),
            pltpu.SMEM((1,), jnp.int32),
            pltpu.VMEM((blocks + 2, HEAD + steps, WIDE), bf16),
            pltpu.VMEM((blocks + 2, HEAD + steps, 8 * BLK), fp8),
            pltpu.VMEM((pairs, HALF * BLK, WIDE), bf16),
            pltpu.VMEM((pairs, 2 * CORR * BLK, WIDE), fp8),
            pltpu.VMEM((pairs, BLK, WIDE), bf16),
            pltpu.VMEM((pairs, LEAD + steps, WIDE), f32),
            pltpu.VMEM((pairs, LEAD + steps, WIDE), f32),
            pltpu.VMEM((blocks + 2, BLK, BLK), f32),
            pltpu.VMEM((blocks + 2, GEO, BLK), f32),
            pltpu.SemaphoreType.DMA((count,)),
            pltpu.SemaphoreType.DMA((count,)),
            pltpu.SemaphoreType.DMA((blocks + 3,)),
        ],
        compiler_params=pltpu.CompilerParams(
            collective_id=0, has_side_effects=True, vmem_limit_bytes=60 * 1024 * 1024
        ),
    )(near_list[0].T, pair_count, *given)


def solution(mesh):
    in_specs = (
        P("freq", ("grp", "panel")),
        P(None, ("grp", "panel")),
        P(("grp", "panel"), None, None),
        P(("grp", "panel")),
    )
    out_specs = P("freq", ("grp", "panel"))
    return jax.shard_map(
        per_device, mesh=mesh, in_specs=in_specs, out_specs=out_specs, check_vma=False
    )
```

```python
import math

import jax
import jax.numpy as jnp
from jax import lax
from jax.experimental import pallas as pl
from jax.experimental.pallas import tpu as pltpu
from jax.sharding import PartitionSpec as P

NT = 1024
BLK = 128
GEO = 8
TAIL = 24
HEAD = 32
PAD = 8
START = PAD + HEAD
LEAD = 16
HALF = 12
CORR = 8
FIXED = 5
WIDE = 2 * BLK

SCALE = 512.0
FIELD_UP = 32.0
LOW_UP = 8192.0
TERM_UP = 256.0

damping = 0.999
time_step = 0.5
core_square = 0.01

bf16 = jnp.bfloat16
fp8 = jnp.float8_e4m3fn
f32 = jnp.float32


def product(x, y):
    return jnp.dot(x, y, preferred_element_type=f32)


def split(v):
    hi = v.astype(bf16)
    return hi, v - hi.astype(f32)


def turn(geometry):
    return jnp.concatenate([geometry] * (BLK // GEO), axis=0).T


def spread(ext, pair_data, four_data, c, first, rows):
    for n in range(4):
        v = ext[c, PAD + first - n : PAD + first - n + rows, :]
        hi, low = split(v)
        if n < 2:
            pair_data[c, first : first + rows, n * BLK : (n + 1) * BLK] = hi
        four_data[c, first : first + rows, n * BLK : (n + 1) * BLK] = (v * FIELD_UP).astype(fp8)
        four_data[c, first : first + rows, (4 + n) * BLK : (5 + n) * BLK] = (low * LOW_UP).astype(fp8)


def fill(main, fine, sample, p, theirs, mine):
    square = jnp.full((BLK, BLK), core_square, f32)
    for a in range(3):
        diff = theirs[:, a : a + 1] - mine[a : a + 1, :]
        square = square + diff * diff
    dist = jnp.sqrt(square)
    x = dist * (1.0 / time_step)
    term = jnp.exp(-x) * (SCALE / (4.0 * math.pi)) / dist
    hi, low = split(term * jnp.exp(-damping * x))
    sample[p, :, :BLK] = hi
    sample[p, :, BLK:] = low.astype(bf16)
    for n in range(TAIL):
        side, place = divmod(n, HALF)
        hi, low = split(term)
        main[p, place * BLK : (place + 1) * BLK, side * BLK : (side + 1) * BLK] = hi
        if n < 2 * CORR:
            side, place = divmod(n, CORR)
            first = (place // 4 * 8 + place % 4) * BLK
            lanes = slice(side * BLK, (side + 1) * BLK)
            fine[p, first : first + BLK, lanes] = (low * TERM_UP).astype(fp8)
            fine[p, first + 4 * BLK : first + 5 * BLK, lanes] = term.astype(fp8)
        if n + 1 < TAIL:
            term = term * (x * (1.0 / (n + 1)))


def contract(pair_data, four_data, main, fine, wide, narrow, p, c, first, last):
    rows = last - first
    total = None
    for k in range(HALF // 2):
        start = HEAD - LEAD + first - 2 * k
        term = product(pair_data[c, start : start + rows, :], main[p, k * WIDE : (k + 1) * WIDE, :])
        total = term if total is None else total + term
    wide[p, first:last, :] = total
    total = None
    for k in range(CORR // 4):
        start = HEAD - LEAD + first - 4 * k
        term = product(four_data[c, start : start + rows, :], fine[p, k * 8 * BLK : (k + 1) * 8 * BLK, :])
        total = term if total is None else total + term
    narrow[p, first:last, :] = total


def gather(wide, narrow, p, first, last):
    a, b = LEAD + first, LEAD + last
    low = narrow[p, a:b, :BLK] + narrow[p, a - CORR : b - CORR, BLK:]
    high = wide[p, a:b, :BLK] + wide[p, a - HALF : b - HALF, BLK:]
    return high * (1.0 / SCALE) + low * (1.0 / (SCALE * FIELD_UP * TERM_UP))


def operator(
    list_hbm,
    count_hbm,
    traces_ref,
    xyz_hbm,
    out_ref,
    ext,
    head,
    slots,
    relay,
    corner,
    sums,
    xyz_ref,
    list_ref,
    count_ref,
    pair_data,
    four_data,
    main,
    fine,
    sample,
    wide,
    narrow,
    turned,
    shape,
    send,
    recv,
    load,
):
    steps, width = traces_ref.shape
    blocks = width // BLK
    geo = START + steps
    groups = lax.axis_size("freq")
    shards = lax.axis_size("panel")
    position = lax.axis_index("freq")
    shard = lax.axis_index("panel")
    pairs = list_ref.shape[1]
    rows = steps + LEAD

    def device(ahead, side):
        return {
            "freq": lax.rem(position + ahead + groups, groups),
            "panel": lax.rem(shard + side + shards, shards),
        }

    def remote(i, ahead, side, source, target):
        return pltpu.make_async_remote_copy(
            src_ref=source,
            dst_ref=target,
            send_sem=send.at[i],
            recv_sem=recv.at[i],
            device_id=device(ahead, side),
            device_id_type=pl.DeviceIdType.MESH,
        )

    peers = [(0, 1), (0, -1)] + [(s, 0) for s in range(1, groups)]
    barrier = pltpu.get_barrier_semaphore()
    for s, d in peers:
        pl.semaphore_signal(
            barrier, inc=1, device_id=device(s, d), device_id_type=pl.DeviceIdType.MESH
        )
    loads = [
        pltpu.make_async_copy(
            traces_ref.at[:, pl.ds(b * BLK, BLK)],
            ext.at[b + 1, pl.ds(START, steps)],
            load.at[b],
        )
        for b in range(blocks)
    ]
    loads.append(pltpu.make_async_copy(xyz_hbm, xyz_ref, load.at[blocks]))
    loads.append(pltpu.make_async_copy(list_hbm, list_ref, load.at[blocks + 1]))
    loads.append(pltpu.make_async_copy(count_hbm, count_ref, load.at[blocks + 2]))
    for copy in loads:
        copy.start()

    own = pl.ds(START, steps)
    spot = pl.ds(geo, GEO)
    middle = pl.ds(1, blocks)
    turns = [remote(0, 1, 0, ext.at[middle, pl.ds(geo - TAIL, TAIL + GEO)], head)]
    for s in range(2, groups):
        turns.append(remote(s - 1, s, 0, ext.at[middle, spot], slots.at[s]))
    after = groups - 1
    marks = [
        remote(after, 0, 1, ext.at[blocks, spot], ext.at[0, spot]),
        remote(after + 1, 0, -1, ext.at[1, spot], ext.at[blocks + 1, spot]),
    ]
    edges = [
        remote(after + 2, 0, 1, ext.at[blocks, own], ext.at[0, own]),
        remote(after + 3, 0, -1, ext.at[1, own], ext.at[blocks + 1, own]),
    ]
    relays = [
        remote(after + 4, 0, 1, relay.at[1], corner.at[0]),
        remote(after + 5, 0, -1, relay.at[0], corner.at[1]),
    ]

    times = position * steps + lax.broadcasted_iota(jnp.int32, (steps, BLK), 0)
    weight = jnp.exp(times.astype(f32) * math.log(damping))
    weight = jnp.where(times % 2 == 0, weight, -weight)
    for copy in loads[blocks:]:
        copy.wait()
    for b in range(blocks):
        loads[b].wait()
        part = jnp.sum(weight * ext[b + 1, START:geo, :], axis=0, keepdims=True)
        ext[b + 1, geo : geo + 3, :] = xyz_ref[:, b * BLK : (b + 1) * BLK]
        ext[b + 1, geo + 3 : geo + 4, :] = part
        ext[b + 1, geo + 4 : geo + GEO, :] = jnp.zeros((GEO - 4, BLK), f32)

    pl.semaphore_wait(barrier, len(peers))
    for copy in turns + marks + edges:
        copy.start()

    ext[:, :START, :] = jnp.zeros((blocks + 2, START, BLK), f32)
    for c in range(1, blocks + 1):
        spread(ext, pair_data, four_data, c, HEAD, steps)
        shape[c] = ext[c, geo : geo + GEO, :]
        turned[c] = turn(shape[c])
    fixed = [(n, n + 1) for n in range(blocks)] + [(0, 0), (blocks - 1, blocks + 1)]
    for p, (r, c) in enumerate(fixed[:blocks]):
        fill(main, fine, sample, p, turned[c], shape[r + 1])
        contract(pair_data, four_data, main, fine, wide, narrow, p, c, HEAD, rows)

    for copy in marks:
        copy.wait()
    for c in (0, blocks + 1):
        shape[c] = ext[c, geo : geo + GEO, :]
        turned[c] = turn(shape[c])
    order = [(jnp.int32(r), jnp.int32(c)) for r, c in fixed]
    order += [(list_ref[0, p], list_ref[1, p]) for p in range(len(fixed), pairs)]
    for p in range(blocks, pairs):
        r, c = order[p] if p >= len(fixed) else fixed[p]
        fill(main, fine, sample, p, turned[c], shape[r + 1])

    pick = lax.broadcasted_iota(jnp.int32, (2 * GEO, BLK), 0)

    def place(c, total):
        total = jnp.broadcast_to(total, (2 * GEO, BLK))
        hi, low = split(total)
        sums[c] = jnp.where(pick == 0, total, jnp.where(pick == 1, low, 0.0)).astype(bf16)

    around = jnp.where(position == 0, math.exp(NT * math.log(damping)), 1.0)
    for copy in turns:
        copy.wait()
    for c in range(1, blocks + 1):
        before = head[c - 1, :TAIL, :] * around
        total = shape[c, 3:4, :] + head[c - 1, TAIL + 3 : TAIL + 4, :]
        for s in range(2, groups):
            total = total + slots[s, c - 1, 3:4, :]
        ext[c, START - TAIL : START, :] = before
        place(c, total)
        if c == 1 or c == blocks:
            relay[c // blocks, :TAIL, :] = before
            relay[c // blocks, TAIL:, :] = jnp.broadcast_to(total, (GEO, BLK))
    for copy in relays:
        copy.start()

    local = lax.broadcasted_iota(jnp.int32, (steps, BLK), 0)
    growth = jnp.exp((position * steps + local).astype(f32) * -math.log(damping)) / (NT * SCALE)
    growth = jnp.where(local % 2 == 0, -growth, growth)

    def whole(p, c):
        both = product(sums[c], sample[p])
        rank = both[0:1, :BLK] + (both[1:2, :BLK] + both[0:1, BLK:])
        return gather(wide, narrow, p, 0, steps) + growth * rank

    for c in range(1, blocks + 1):
        spread(ext, pair_data, four_data, c, 0, HEAD + LEAD)
    for p in range(blocks):
        contract(pair_data, four_data, main, fine, wide, narrow, p, p + 1, 0, HEAD)
    for p in range(blocks):
        out_ref[:, p * BLK : (p + 1) * BLK] = whole(p, p + 1)

    for n, c in enumerate((0, blocks + 1)):
        edges[n].wait()
        spread(ext, pair_data, four_data, c, HEAD, steps)
        contract(pair_data, four_data, main, fine, wide, narrow, blocks + n, c, HEAD, rows)
    for n, c in enumerate((0, blocks + 1)):
        relays[n].wait()
        ext[c, START - TAIL : START, :] = corner[n, :TAIL, :]
        place(c, corner[n, TAIL : TAIL + 1, :])
        spread(ext, pair_data, four_data, c, 0, HEAD + LEAD)
        contract(pair_data, four_data, main, fine, wide, narrow, blocks + n, c, 0, HEAD)
    for p in range(len(fixed), pairs):
        contract(pair_data, four_data, main, fine, wide, narrow, p, order[p][1], 0, rows)
    for p in range(blocks, len(fixed)):
        r, c = fixed[p]
        lanes = slice(r * BLK, (r + 1) * BLK)
        out_ref[:, lanes] = out_ref[:, lanes] + whole(p, c)
    for p in range(len(fixed), pairs):
        total = whole(p, order[p][1])
        target = jnp.where(p < count_ref[0], order[p][0], blocks)
        for r in range(blocks):
            lanes = slice(r * BLK, (r + 1) * BLK)
            out_ref[:, lanes] = out_ref[:, lanes] + jnp.where(target == r, total, 0.0)


def per_device(traces, centroids, near_list, pair_count):
    steps, width = traces.shape
    blocks = width // BLK
    pairs = near_list.shape[1]
    groups = lax.axis_size("freq")
    count = 5 + groups
    hbm = pl.BlockSpec(memory_space=pltpu.HBM)
    given = [pltpu.with_memory_space_constraint(v, pltpu.HBM) for v in (traces, centroids)]
    return pl.pallas_call(
        operator,
        out_shape=pltpu.VMEM((steps, width), f32),
        in_specs=[hbm] * 4,
        out_specs=pl.BlockSpec(memory_space=pltpu.VMEM),
        scratch_shapes=[
            pltpu.VMEM((blocks + 2, START + steps + GEO, BLK), f32),
            pltpu.VMEM((blocks, TAIL + GEO, BLK), f32),
            pltpu.VMEM((groups, blocks, GEO, BLK), f32),
            pltpu.VMEM((2, TAIL + GEO, BLK), f32),
            pltpu.VMEM((2, TAIL + GEO, BLK), f32),
            pltpu.VMEM((blocks + 2, 2 * GEO, BLK), bf16),
            pltpu.VMEM((3, width), f32),
            pltpu.SMEM((2, pairs), jnp.int32),
            pltpu.SMEM((1,), jnp.int32),
            pltpu.VMEM((blocks + 2, HEAD + steps, WIDE), bf16),
            pltpu.VMEM((blocks + 2, HEAD + steps, 8 * BLK), fp8),
            pltpu.VMEM((pairs, HALF * BLK, WIDE), bf16),
            pltpu.VMEM((pairs, 2 * CORR * BLK, WIDE), fp8),
            pltpu.VMEM((pairs, BLK, WIDE), bf16),
            pltpu.VMEM((pairs, LEAD + steps, WIDE), f32),
            pltpu.VMEM((pairs, LEAD + steps, WIDE), f32),
            pltpu.VMEM((blocks + 2, BLK, BLK), f32),
            pltpu.VMEM((blocks + 2, GEO, BLK), f32),
            pltpu.SemaphoreType.DMA((count,)),
            pltpu.SemaphoreType.DMA((count,)),
            pltpu.SemaphoreType.DMA((blocks + 3,)),
        ],
        compiler_params=pltpu.CompilerParams(
            collective_id=0, has_side_effects=True, vmem_limit_bytes=60 * 1024 * 1024
        ),
    )(near_list[0].T, pair_count, *given)


def solution(mesh):
    in_specs = (
        P("freq", ("grp", "panel")),
        P(None, ("grp", "panel")),
        P(("grp", "panel"), None, None),
        P(("grp", "panel")),
    )
    out_specs = P("freq", ("grp", "panel"))
    return jax.shard_map(
        per_device, mesh=mesh, in_specs=in_specs, out_specs=out_specs, check_vma=False
    )
```

```python
import math

import jax
import jax.numpy as jnp
from jax import lax
from jax.experimental import pallas as pl
from jax.experimental.pallas import tpu as pltpu
from jax.sharding import PartitionSpec as P

NT = 1024
BLK = 128
GEO = 8
TAIL = 24
HEAD = 32
PAD = 8
START = PAD + HEAD
LEAD = 16
HALF = 12
CORR = 8
FIXED = 5
WIDE = 2 * BLK

SCALE = 512.0
FIELD_UP = 32.0
LOW_UP = 8192.0
TERM_UP = 256.0

damping = 0.999
time_step = 0.5
core_square = 0.01

bf16 = jnp.bfloat16
fp8 = jnp.float8_e4m3fn
f32 = jnp.float32


def product(x, y):
    return jnp.dot(x, y, preferred_element_type=f32)


def split(v):
    hi = v.astype(bf16)
    return hi, v - hi.astype(f32)


def turn(geometry):
    return jnp.concatenate([geometry] * (BLK // GEO), axis=0).T


def spread(ext, pair_data, four_data, c, first, rows):
    for n in range(4):
        v = ext[c, PAD + first - n : PAD + first - n + rows, :]
        hi, low = split(v)
        if n < 2:
            pair_data[c, first : first + rows, n * BLK : (n + 1) * BLK] = hi
        four_data[c, first : first + rows, n * BLK : (n + 1) * BLK] = (v * FIELD_UP).astype(fp8)
        four_data[c, first : first + rows, (4 + n) * BLK : (5 + n) * BLK] = (low * LOW_UP).astype(fp8)


def fill(main, fine, sample, p, theirs, mine):
    square = jnp.full((BLK, BLK), core_square, f32)
    for a in range(3):
        diff = theirs[:, a : a + 1] - mine[a : a + 1, :]
        square = square + diff * diff
    dist = jnp.sqrt(square)
    x = dist * (1.0 / time_step)
    term = jnp.exp(-x) * (SCALE / (4.0 * math.pi)) / dist
    hi, low = split(term * jnp.exp(-damping * x))
    sample[p, :, :BLK] = hi
    sample[p, :, BLK:] = low.astype(bf16)
    for n in range(TAIL):
        side, place = divmod(n, HALF)
        hi, low = split(term)
        main[p, place * BLK : (place + 1) * BLK, side * BLK : (side + 1) * BLK] = hi
        if n < 2 * CORR:
            side, place = divmod(n, CORR)
            first = (place // 4 * 8 + place % 4) * BLK
            lanes = slice(side * BLK, (side + 1) * BLK)
            fine[p, first : first + BLK, lanes] = (low * TERM_UP).astype(fp8)
            fine[p, first + 4 * BLK : first + 5 * BLK, lanes] = term.astype(fp8)
        if n + 1 < TAIL:
            term = term * (x * (1.0 / (n + 1)))


def contract(pair_data, four_data, main, fine, wide, narrow, p, c, first, last):
    rows = last - first
    total = None
    for k in range(HALF // 2):
        start = HEAD - LEAD + first - 2 * k
        term = product(pair_data[c, start : start + rows, :], main[p, k * WIDE : (k + 1) * WIDE, :])
        total = term if total is None else total + term
    wide[p, first:last, :] = total
    total = None
    for k in range(CORR // 4):
        start = HEAD - LEAD + first - 4 * k
        term = product(four_data[c, start : start + rows, :], fine[p, k * 8 * BLK : (k + 1) * 8 * BLK, :])
        total = term if total is None else total + term
    narrow[p, first:last, :] = total


def gather(wide, narrow, p, first, last):
    a, b = LEAD + first, LEAD + last
    low = narrow[p, a:b, :BLK] + narrow[p, a - CORR : b - CORR, BLK:]
    high = wide[p, a:b, :BLK] + wide[p, a - HALF : b - HALF, BLK:]
    return high * (1.0 / SCALE) + low * (1.0 / (SCALE * FIELD_UP * TERM_UP))


def operator(
    list_hbm,
    count_hbm,
    traces_ref,
    xyz_hbm,
    out_ref,
    ext,
    head,
    slots,
    relay,
    corner,
    sums,
    xyz_ref,
    list_ref,
    count_ref,
    pair_data,
    four_data,
    main,
    fine,
    sample,
    wide,
    narrow,
    turned,
    shape,
    send,
    recv,
    load,
    ready,
):
    steps, width = traces_ref.shape
    blocks = width // BLK
    geo = START + steps
    groups = lax.axis_size("freq")
    shards = lax.axis_size("panel")
    position = lax.axis_index("freq")
    shard = lax.axis_index("panel")
    pairs = list_ref.shape[1]
    rows = steps + LEAD

    def device(ahead, side):
        return {
            "freq": lax.rem(position + ahead + groups, groups),
            "panel": lax.rem(shard + side + shards, shards),
        }

    def remote(i, ahead, side, source, target):
        return pltpu.make_async_remote_copy(
            src_ref=source,
            dst_ref=target,
            send_sem=send.at[i],
            recv_sem=recv.at[i],
            device_id=device(ahead, side),
            device_id_type=pl.DeviceIdType.MESH,
        )

    def signal(semaphore, ahead, side):
        pl.semaphore_signal(
            semaphore,
            inc=1,
            device_id=device(ahead, side),
            device_id_type=pl.DeviceIdType.MESH,
        )

    barrier = pltpu.get_barrier_semaphore()
    signal(barrier, 0, 1)
    signal(barrier, 0, -1)
    for s in range(1, groups):

        @pl.when(position + s < groups)
        def _():
            signal(barrier, s, 0)

    loads = [
        pltpu.make_async_copy(
            traces_ref.at[:, pl.ds(b * BLK, BLK)],
            ext.at[b + 1, pl.ds(START, steps)],
            load.at[b],
        )
        for b in range(blocks)
    ]
    loads.append(pltpu.make_async_copy(xyz_hbm, xyz_ref, load.at[blocks]))
    loads.append(pltpu.make_async_copy(list_hbm, list_ref, load.at[blocks + 1]))
    loads.append(pltpu.make_async_copy(count_hbm, count_ref, load.at[blocks + 2]))
    for copy in loads:
        copy.start()

    own = pl.ds(START, steps)
    spot = pl.ds(geo, GEO)
    middle = pl.ds(1, blocks)
    turns = [remote(0, 1, 0, ext.at[middle, pl.ds(geo - TAIL, TAIL + GEO)], head)]
    for s in range(2, groups):
        turns.append(remote(s - 1, s, 0, ext.at[middle, spot], slots.at[s]))
    after = groups - 1
    marks = [
        remote(after, 0, 1, ext.at[blocks, spot], ext.at[0, spot]),
        remote(after + 1, 0, -1, ext.at[1, spot], ext.at[blocks + 1, spot]),
    ]
    edges = [
        remote(after + 2, 0, 1, ext.at[blocks, own], ext.at[0, own]),
        remote(after + 3, 0, -1, ext.at[1, own], ext.at[blocks + 1, own]),
    ]
    relays = [
        remote(after + 4, 0, 1, relay.at[1], corner.at[0]),
        remote(after + 5, 0, -1, relay.at[0], corner.at[1]),
    ]

    times = position * steps + lax.broadcasted_iota(jnp.int32, (steps, BLK), 0)
    weight = jnp.exp(times.astype(f32) * math.log(damping))
    weight = jnp.where(times % 2 == 0, weight, -weight)
    for copy in loads[blocks:]:
        copy.wait()
    for b in range(blocks):
        loads[b].wait()
        part = jnp.sum(weight * ext[b + 1, START:geo, :], axis=0, keepdims=True)
        ext[b + 1, geo : geo + 3, :] = xyz_ref[:, b * BLK : (b + 1) * BLK]
        ext[b + 1, geo + 3 : geo + 4, :] = part
        ext[b + 1, geo + 4 : geo + GEO, :] = jnp.zeros((GEO - 4, BLK), f32)

    pl.semaphore_wait(barrier, 2 + position)
    for copy in marks + edges:
        copy.start()
    for s in range(1, groups):

        @pl.when(position >= s)
        def _():
            signal(ready.at[s], -s, 0)

        @pl.when(position + s >= groups)
        def _():
            turns[s - 1].start()


    ext[:, :START, :] = jnp.zeros((blocks + 2, START, BLK), f32)
    for c in range(1, blocks + 1):
        spread(ext, pair_data, four_data, c, HEAD, steps)
        shape[c] = ext[c, geo : geo + GEO, :]
        turned[c] = turn(shape[c])
    fixed = [(n, n + 1) for n in range(blocks)] + [(0, 0), (blocks - 1, blocks + 1)]
    for p, (r, c) in enumerate(fixed[:blocks]):
        fill(main, fine, sample, p, turned[c], shape[r + 1])
        contract(pair_data, four_data, main, fine, wide, narrow, p, c, HEAD, rows)

    for s in range(1, groups):

        @pl.when(position + s < groups)
        def _():
            pl.semaphore_wait(ready.at[s], 1)
            turns[s - 1].start()

    for copy in marks:
        copy.wait()
    for c in (0, blocks + 1):
        shape[c] = ext[c, geo : geo + GEO, :]
        turned[c] = turn(shape[c])
    order = [(jnp.int32(r), jnp.int32(c)) for r, c in fixed]
    order += [(list_ref[0, p], list_ref[1, p]) for p in range(len(fixed), pairs)]
    for p in range(blocks, pairs):
        r, c = order[p] if p >= len(fixed) else fixed[p]
        fill(main, fine, sample, p, turned[c], shape[r + 1])

    pick = lax.broadcasted_iota(jnp.int32, (2 * GEO, BLK), 0)

    def place(c, total):
        total = jnp.broadcast_to(total, (2 * GEO, BLK))
        hi, low = split(total)
        sums[c] = jnp.where(pick == 0, total, jnp.where(pick == 1, low, 0.0)).astype(bf16)

    around = jnp.where(position == 0, math.exp(NT * math.log(damping)), 1.0)
    for copy in turns:
        copy.wait()
    for c in range(1, blocks + 1):
        before = head[c - 1, :TAIL, :] * around
        total = shape[c, 3:4, :] + head[c - 1, TAIL + 3 : TAIL + 4, :]
        for s in range(2, groups):
            total = total + slots[s, c - 1, 3:4, :]
        ext[c, START - TAIL : START, :] = before
        place(c, total)
        if c == 1 or c == blocks:
            relay[c // blocks, :TAIL, :] = before
            relay[c // blocks, TAIL:, :] = jnp.broadcast_to(total, (GEO, BLK))
    for copy in relays:
        copy.start()

    local = lax.broadcasted_iota(jnp.int32, (steps, BLK), 0)
    growth = jnp.exp((position * steps + local).astype(f32) * -math.log(damping)) / (NT * SCALE)
    growth = jnp.where(local % 2 == 0, -growth, growth)

    def whole(p, c):
        both = product(sums[c], sample[p])
        rank = both[0:1, :BLK] + (both[1:2, :BLK] + both[0:1, BLK:])
        return gather(wide, narrow, p, 0, steps) + growth * rank

    for c in range(1, blocks + 1):
        spread(ext, pair_data, four_data, c, 0, HEAD + LEAD)
    for p in range(blocks):
        contract(pair_data, four_data, main, fine, wide, narrow, p, p + 1, 0, HEAD)
    for p in range(blocks):
        out_ref[:, p * BLK : (p + 1) * BLK] = whole(p, p + 1)

    for n, c in enumerate((0, blocks + 1)):
        edges[n].wait()
        spread(ext, pair_data, four_data, c, HEAD, steps)
        contract(pair_data, four_data, main, fine, wide, narrow, blocks + n, c, HEAD, rows)
    for n, c in enumerate((0, blocks + 1)):
        relays[n].wait()
        ext[c, START - TAIL : START, :] = corner[n, :TAIL, :]
        place(c, corner[n, TAIL : TAIL + 1, :])
        spread(ext, pair_data, four_data, c, 0, HEAD + LEAD)
        contract(pair_data, four_data, main, fine, wide, narrow, blocks + n, c, 0, HEAD)
    for p in range(len(fixed), pairs):
        contract(pair_data, four_data, main, fine, wide, narrow, p, order[p][1], 0, rows)
    for p in range(blocks, len(fixed)):
        r, c = fixed[p]
        lanes = slice(r * BLK, (r + 1) * BLK)
        out_ref[:, lanes] = out_ref[:, lanes] + whole(p, c)
    for p in range(len(fixed), pairs):
        total = whole(p, order[p][1])
        target = jnp.where(p < count_ref[0], order[p][0], blocks)
        for r in range(blocks):
            lanes = slice(r * BLK, (r + 1) * BLK)
            out_ref[:, lanes] = out_ref[:, lanes] + jnp.where(target == r, total, 0.0)


def per_device(traces, centroids, near_list, pair_count):
    steps, width = traces.shape
    blocks = width // BLK
    pairs = near_list.shape[1]
    groups = lax.axis_size("freq")
    count = 5 + groups
    hbm = pl.BlockSpec(memory_space=pltpu.HBM)
    given = [pltpu.with_memory_space_constraint(v, pltpu.HBM) for v in (traces, centroids)]
    return pl.pallas_call(
        operator,
        out_shape=pltpu.VMEM((steps, width), f32),
        in_specs=[hbm] * 4,
        out_specs=pl.BlockSpec(memory_space=pltpu.VMEM),
        scratch_shapes=[
            pltpu.VMEM((blocks + 2, START + steps + GEO, BLK), f32),
            pltpu.VMEM((blocks, TAIL + GEO, BLK), f32),
            pltpu.VMEM((groups, blocks, GEO, BLK), f32),
            pltpu.VMEM((2, TAIL + GEO, BLK), f32),
            pltpu.VMEM((2, TAIL + GEO, BLK), f32),
            pltpu.VMEM((blocks + 2, 2 * GEO, BLK), bf16),
            pltpu.VMEM((3, width), f32),
            pltpu.SMEM((2, pairs), jnp.int32),
            pltpu.SMEM((1,), jnp.int32),
            pltpu.VMEM((blocks + 2, HEAD + steps, WIDE), bf16),
            pltpu.VMEM((blocks + 2, HEAD + steps, 8 * BLK), fp8),
            pltpu.VMEM((pairs, HALF * BLK, WIDE), bf16),
            pltpu.VMEM((pairs, 2 * CORR * BLK, WIDE), fp8),
            pltpu.VMEM((pairs, BLK, WIDE), bf16),
            pltpu.VMEM((pairs, LEAD + steps, WIDE), f32),
            pltpu.VMEM((pairs, LEAD + steps, WIDE), f32),
            pltpu.VMEM((blocks + 2, BLK, BLK), f32),
            pltpu.VMEM((blocks + 2, GEO, BLK), f32),
            pltpu.SemaphoreType.DMA((count,)),
            pltpu.SemaphoreType.DMA((count,)),
            pltpu.SemaphoreType.DMA((blocks + 3,)),
            pltpu.SemaphoreType.REGULAR((groups,)),
        ],
        compiler_params=pltpu.CompilerParams(
            collective_id=0, has_side_effects=True, vmem_limit_bytes=60 * 1024 * 1024
        ),
    )(near_list[0].T, pair_count, *given)


def solution(mesh):
    in_specs = (
        P("freq", ("grp", "panel")),
        P(None, ("grp", "panel")),
        P(("grp", "panel"), None, None),
        P(("grp", "panel")),
    )
    out_specs = P("freq", ("grp", "panel"))
    return jax.shard_map(
        per_device, mesh=mesh, in_specs=in_specs, out_specs=out_specs, check_vma=False
    )
```

```python
import math

import jax
import jax.numpy as jnp
from jax import lax
from jax.experimental import pallas as pl
from jax.experimental.pallas import tpu as pltpu
from jax.sharding import PartitionSpec as P

NT = 1024
BLK = 128
GEO = 8
TAIL = 24
HEAD = 32
PAD = 8
START = PAD + HEAD
LEAD = 16
HALF = 12
CORR = 6
FIXED = 5
WIDE = 2 * BLK

SCALE = 512.0
FIELD_UP = 32.0
LOW_UP = 8192.0
TERM_UP = 256.0

damping = 0.999
time_step = 0.5
core_square = 0.01

bf16 = jnp.bfloat16
fp8 = jnp.float8_e4m3fn
f32 = jnp.float32


def product(x, y):
    return jnp.dot(x, y, preferred_element_type=f32)


def split(v):
    hi = v.astype(bf16)
    return hi, v - hi.astype(f32)


def turn(geometry):
    return jnp.concatenate([geometry] * (BLK // GEO), axis=0).T


def spread(ext, pair_data, four_data, c, first, rows):
    for n in range(4):
        v = ext[c, PAD + first - n : PAD + first - n + rows, :]
        hi, low = split(v)
        if n < 2:
            pair_data[c, first : first + rows, n * BLK : (n + 1) * BLK] = hi
        at = (n // 2 * 4 + n % 2) * BLK
        four_data[c, first : first + rows, at : at + BLK] = (v * FIELD_UP).astype(fp8)
        at = at + 2 * BLK
        four_data[c, first : first + rows, at : at + BLK] = (low * LOW_UP).astype(fp8)


def fill(main, fine, sample, p, theirs, mine):
    square = jnp.full((BLK, BLK), core_square, f32)
    for a in range(3):
        diff = theirs[:, a : a + 1] - mine[a : a + 1, :]
        square = square + diff * diff
    dist = jnp.sqrt(square)
    x = dist * (1.0 / time_step)
    term = jnp.exp(-x) * (SCALE / (4.0 * math.pi)) / dist
    hi, low = split(term * jnp.exp(-damping * x))
    sample[p, :, :BLK] = hi
    sample[p, :, BLK:] = low.astype(bf16)
    for n in range(TAIL):
        side, place = divmod(n, HALF)
        hi, low = split(term)
        main[p, place * BLK : (place + 1) * BLK, side * BLK : (side + 1) * BLK] = hi
        if n < 2 * CORR:
            side, place = divmod(n, CORR)
            first = (place // 2 * 4 + place % 2) * BLK
            lanes = slice(side * BLK, (side + 1) * BLK)
            fine[p, first : first + BLK, lanes] = (low * TERM_UP).astype(fp8)
            fine[p, first + 2 * BLK : first + 3 * BLK, lanes] = term.astype(fp8)
        if n + 1 < TAIL:
            term = term * (x * (1.0 / (n + 1)))


def contract(pair_data, four_data, main, fine, wide, narrow, p, c, first, last):
    rows = last - first
    total = None
    for k in range(HALF // 2):
        start = HEAD - LEAD + first - 2 * k
        term = product(pair_data[c, start : start + rows, :], main[p, k * WIDE : (k + 1) * WIDE, :])
        total = term if total is None else total + term
    wide[p, first:last, :] = total
    total = None
    for k in range(0, CORR, 4):
        start = HEAD - LEAD + first - k
        depth = 2 * min(4, CORR - k) * BLK
        term = product(
            four_data[c, start : start + rows, :depth], fine[p, 2 * k * BLK : 2 * k * BLK + depth, :]
        )
        total = term if total is None else total + term
    narrow[p, first:last, :] = total


def gather(wide, narrow, p, first, last):
    a, b = LEAD + first, LEAD + last
    low = narrow[p, a:b, :BLK] + narrow[p, a - CORR : b - CORR, BLK:]
    high = wide[p, a:b, :BLK] + wide[p, a - HALF : b - HALF, BLK:]
    return high * (1.0 / SCALE) + low * (1.0 / (SCALE * FIELD_UP * TERM_UP))


def operator(
    list_hbm,
    count_hbm,
    traces_ref,
    xyz_hbm,
    out_ref,
    ext,
    head,
    slots,
    mark,
    parts,
    corner,
    sums,
    xyz_ref,
    list_ref,
    count_ref,
    pair_data,
    four_data,
    main,
    fine,
    sample,
    wide,
    narrow,
    turned,
    shape,
    send,
    recv,
    load,
    ready,
):
    steps, width = traces_ref.shape
    blocks = width // BLK
    geo = START + steps
    groups = lax.axis_size("freq")
    shards = lax.axis_size("panel")
    position = lax.axis_index("freq")
    shard = lax.axis_index("panel")
    pairs = list_ref.shape[1]
    rows = steps + LEAD

    def device(ahead, side):
        return {
            "freq": lax.rem(position + ahead + groups, groups),
            "panel": lax.rem(shard + side + shards, shards),
        }

    def signal(semaphore, ahead, side):
        pl.semaphore_signal(
            semaphore,
            inc=1,
            device_id=device(ahead, side),
            device_id_type=pl.DeviceIdType.MESH,
        )

    barrier = pltpu.get_barrier_semaphore()
    signal(barrier, 0, 1)
    signal(barrier, 0, -1)
    sides = (0, 1, -1)
    for s in range(1, groups):

        @pl.when(position + s < groups)
        def _():
            for d in sides:
                signal(barrier, s, d)

    loads = [pltpu.make_async_copy(xyz_hbm, xyz_ref, load.at[blocks])]
    loads += [
        pltpu.make_async_copy(
            traces_ref.at[:, pl.ds(b * BLK, BLK)],
            ext.at[b + 1, pl.ds(START, steps)],
            load.at[b],
        )
        for b in range(blocks)
    ]
    loads.append(pltpu.make_async_copy(list_hbm, list_ref, load.at[blocks + 1]))
    loads.append(pltpu.make_async_copy(count_hbm, count_ref, load.at[blocks + 2]))
    for copy in loads:
        copy.start()

    made = []

    def remote(ahead, side, source, target):
        i = len(made)
        made.append(i)
        return pltpu.make_async_remote_copy(
            src_ref=source,
            dst_ref=target,
            send_sem=send.at[i],
            recv_sem=recv.at[i],
            device_id=device(ahead, side),
            device_id_type=pl.DeviceIdType.MESH,
        )

    own = pl.ds(START, steps)
    tail = pl.ds(steps - TAIL, TAIL)
    left, right = pl.ds(0, BLK), pl.ds((blocks - 1) * BLK, BLK)
    edges = [
        remote(0, 1, ext.at[blocks, own], ext.at[0, own]),
        remote(0, -1, ext.at[1, own], ext.at[blocks + 1, own]),
    ]
    marks = [
        remote(0, 1, mark.at[blocks - 1], shape.at[0]),
        remote(0, -1, mark.at[0], shape.at[blocks + 1]),
    ]
    tails = [
        remote(1, 0, traces_ref.at[tail, :], head),
        remote(1, 1, traces_ref.at[tail, right], corner.at[0]),
        remote(1, -1, traces_ref.at[tail, left], corner.at[1]),
    ]
    turns = [
        [remote(s, d, parts, slots.at[s, n]) for n, d in enumerate(sides)] for s in range(1, groups)
    ]

    times = position * steps + lax.broadcasted_iota(jnp.int32, (steps, BLK), 0)
    weight = jnp.exp(times.astype(f32) * math.log(damping))
    weight = jnp.where(times % 2 == 0, weight, -weight)

    pl.semaphore_wait(barrier, 2 + len(sides) * position)
    for s in range(1, groups):

        @pl.when(position >= s)
        def _():
            signal(ready.at[s], -s, 0)

    @pl.when(position + 1 >= groups)
    def _():
        for copy in tails:
            copy.start()

    for copy in loads:
        copy.wait()
    parts[blocks:, :] = jnp.zeros((GEO - blocks, BLK), f32)
    for b in range(blocks):
        part = jnp.sum(weight * ext[b + 1, START:geo, :], axis=0, keepdims=True)
        parts[b : b + 1, :] = part
        mark[b, 0:3, :] = xyz_ref[:, b * BLK : (b + 1) * BLK]
        mark[b, 3:4, :] = part
        mark[b, 4:, :] = jnp.zeros((GEO - 4, BLK), f32)
    for copy in marks:
        copy.start()
    for s in range(1, groups):

        @pl.when(position + s >= groups)
        def _():
            for copy in turns[s - 1]:
                copy.start()

    for copy in edges:
        copy.start()

    def up(s):
        @pl.when(position + s < groups)
        def _():
            pl.semaphore_wait(ready.at[s], 1)
            for copy in (tails if s == 1 else []) + turns[s - 1]:
                copy.start()

    ext[:, :START, :] = jnp.zeros((blocks + 2, START, BLK), f32)
    for c in range(1, blocks + 1):
        spread(ext, pair_data, four_data, c, HEAD, steps)
        shape[c] = mark[c - 1]
        turned[c] = turn(shape[c])
    fixed = [(n, n + 1) for n in range(blocks)] + [(0, 0), (blocks - 1, blocks + 1)]
    for p, (r, c) in enumerate(fixed[:blocks]):
        fill(main, fine, sample, p, turned[c], shape[r + 1])
        contract(pair_data, four_data, main, fine, wide, narrow, p, c, HEAD, rows)
        if p == 0:
            up(1)

    for copy in marks:
        copy.wait()
    for c in (0, blocks + 1):
        turned[c] = turn(shape[c])
    order = list(fixed)
    order += [(list_ref[0, p], list_ref[1, p]) for p in range(len(fixed), pairs)]
    for p in range(blocks, pairs):
        r, c = order[p]
        fill(main, fine, sample, p, turned[c], shape[r + 1])

    if groups > 2:
        up(2)
    for n, c in enumerate((0, blocks + 1)):
        edges[n].wait()
        spread(ext, pair_data, four_data, c, HEAD, steps)
        contract(pair_data, four_data, main, fine, wide, narrow, blocks + n, c, HEAD, rows)
    for s in range(3, groups):
        up(s)
    for p in range(len(fixed), pairs):
        contract(pair_data, four_data, main, fine, wide, narrow, p, order[p][1], HEAD, rows)

    def collect(first, last):
        for r in range(blocks):
            total = None
            for p, (row, _) in enumerate(fixed):
                if row == r:
                    term = gather(wide, narrow, p, first, last)
                    total = term if total is None else total + term
            out_ref[first:last, r * BLK : (r + 1) * BLK] = total
        for p in range(len(fixed), pairs):
            total = gather(wide, narrow, p, first, last)
            for r in range(blocks):
                lanes = slice(r * BLK, (r + 1) * BLK)
                out_ref[first:last, lanes] = out_ref[first:last, lanes] + jnp.where(
                    targets[p] == r, total, 0.0
                )

    targets = {
        p: jnp.where(p < count_ref[0], order[p][0], blocks) for p in range(len(fixed), pairs)
    }
    if steps > HEAD:
        collect(HEAD, steps)
    around = jnp.where(position == 0, math.exp(NT * math.log(damping)), 1.0)
    local = lax.broadcasted_iota(jnp.int32, (steps, BLK), 0)
    growth = jnp.exp((position * steps + local).astype(f32) * -math.log(damping)) / (NT * SCALE)
    growth = jnp.where(local % 2 == 0, -growth, growth)
    pick = lax.broadcasted_iota(jnp.int32, (2 * GEO, BLK), 0)

    def follow(c, before):
        ext[c, START - TAIL : START, :] = before * around
        spread(ext, pair_data, four_data, c, 0, HEAD + LEAD)

    tails[0].wait()
    for c in range(1, blocks + 1):
        follow(c, head[:, (c - 1) * BLK : c * BLK])
    for p in range(blocks):
        contract(pair_data, four_data, main, fine, wide, narrow, p, p + 1, 0, HEAD)
    tails[1].wait()
    follow(0, corner[0])
    contract(pair_data, four_data, main, fine, wide, narrow, blocks, 0, 0, HEAD)
    tails[2].wait()
    follow(blocks + 1, corner[1])
    contract(pair_data, four_data, main, fine, wide, narrow, blocks + 1, blocks + 1, 0, HEAD)
    for p in range(len(fixed), pairs):
        contract(pair_data, four_data, main, fine, wide, narrow, p, order[p][1], 0, HEAD)

    for some in turns:
        for copy in some:
            copy.wait()
    for c in range(blocks + 2):
        n, b = (1, blocks - 1) if c == 0 else (2, 0) if c > blocks else (0, c - 1)
        total = shape[c, 3:4, :]
        for s in range(1, groups):
            total = total + slots[s, n, b : b + 1, :]
        total = jnp.broadcast_to(total, (2 * GEO, BLK))
        hi, low = split(total)
        sums[c] = jnp.where(pick == 0, total, jnp.where(pick == 1, low, 0.0)).astype(bf16)

    ranks = []
    for p in range(pairs):
        both = product(sums[order[p][1]], sample[p])
        ranks.append(both[0:1, :BLK] + (both[1:2, :BLK] + both[0:1, BLK:]))
    collect(0, HEAD)
    for r in range(blocks):
        rank = jnp.zeros((1, BLK), f32)
        for p in range(pairs):
            if p < len(fixed):
                rank = rank + ranks[p] if fixed[p][0] == r else rank
            else:
                rank = rank + jnp.where(targets[p] == r, ranks[p], 0.0)
        lanes = slice(r * BLK, (r + 1) * BLK)
        out_ref[:, lanes] = out_ref[:, lanes] + growth * rank


def per_device(traces, centroids, near_list, pair_count):
    steps, width = traces.shape
    blocks = width // BLK
    pairs = near_list.shape[1]
    groups = lax.axis_size("freq")
    count = 4 + 3 * groups
    hbm = pl.BlockSpec(memory_space=pltpu.HBM)
    given = [pltpu.with_memory_space_constraint(v, pltpu.HBM) for v in (traces, centroids)]
    return pl.pallas_call(
        operator,
        out_shape=pltpu.VMEM((steps, width), f32),
        in_specs=[hbm] * 4,
        out_specs=pl.BlockSpec(memory_space=pltpu.VMEM),
        scratch_shapes=[
            pltpu.VMEM((blocks + 2, START + steps, BLK), f32),
            pltpu.VMEM((TAIL, width), f32),
            pltpu.VMEM((groups, 3, GEO, BLK), f32),
            pltpu.VMEM((blocks, GEO, BLK), f32),
            pltpu.VMEM((GEO, BLK), f32),
            pltpu.VMEM((2, TAIL, BLK), f32),
            pltpu.VMEM((blocks + 2, 2 * GEO, BLK), bf16),
            pltpu.VMEM((3, width), f32),
            pltpu.SMEM((2, pairs), jnp.int32),
            pltpu.SMEM((1,), jnp.int32),
            pltpu.VMEM((blocks + 2, HEAD + steps, WIDE), bf16),
            pltpu.VMEM((blocks + 2, HEAD + steps, 8 * BLK), fp8),
            pltpu.VMEM((pairs, HALF * BLK, WIDE), bf16),
            pltpu.VMEM((pairs, 2 * CORR * BLK, WIDE), fp8),
            pltpu.VMEM((pairs, BLK, WIDE), bf16),
            pltpu.VMEM((pairs, LEAD + steps, WIDE), f32),
            pltpu.VMEM((pairs, LEAD + steps, WIDE), f32),
            pltpu.VMEM((blocks + 2, BLK, BLK), f32),
            pltpu.VMEM((blocks + 2, GEO, BLK), f32),
            pltpu.SemaphoreType.DMA((count,)),
            pltpu.SemaphoreType.DMA((count,)),
            pltpu.SemaphoreType.DMA((blocks + 3,)),
            pltpu.SemaphoreType.REGULAR((groups,)),
        ],
        compiler_params=pltpu.CompilerParams(
            collective_id=0, has_side_effects=True, vmem_limit_bytes=60 * 1024 * 1024
        ),
    )(near_list[0].T, pair_count, *given)


def solution(mesh):
    in_specs = (
        P("freq", ("grp", "panel")),
        P(None, ("grp", "panel")),
        P(("grp", "panel"), None, None),
        P(("grp", "panel")),
    )
    out_specs = P("freq", ("grp", "panel"))
    return jax.shard_map(
        per_device, mesh=mesh, in_specs=in_specs, out_specs=out_specs, check_vma=False
    )
```

```python
import math

import jax
import jax.numpy as jnp
from jax import lax
from jax.experimental import pallas as pl
from jax.experimental.pallas import tpu as pltpu
from jax.sharding import PartitionSpec as P

NT = 1024
BLK = 128
GEO = 8
TAIL = 24
HEAD = 32
PAD = 8
START = PAD + HEAD
LEAD = 16
HALF = 12
CORR = 6
FIXED = 5
WIDE = 2 * BLK

SCALE = 512.0
FIELD_UP = 32.0
LOW_UP = 8192.0
TERM_UP = 256.0

damping = 0.999
time_step = 0.5
core_square = 0.01

bf16 = jnp.bfloat16
fp8 = jnp.float8_e4m3fn
f32 = jnp.float32


def product(x, y):
    return jnp.dot(x, y, preferred_element_type=f32)


def split(v):
    hi = v.astype(bf16)
    return hi, v - hi.astype(f32)


def turn(geometry):
    return jnp.concatenate([geometry] * (BLK // GEO), axis=0).T


def spread(ext, pair_data, four_data, c, first, rows):
    for n in range(4):
        v = ext[c, PAD + first - n : PAD + first - n + rows, :]
        hi, low = split(v)
        if n < 2:
            pair_data[c, first : first + rows, n * BLK : (n + 1) * BLK] = hi
        at = (n // 2 * 4 + n % 2) * BLK
        four_data[c, first : first + rows, at : at + BLK] = (v * FIELD_UP).astype(fp8)
        at = at + 2 * BLK
        four_data[c, first : first + rows, at : at + BLK] = (low * LOW_UP).astype(fp8)


def fill(main, fine, sample, p, theirs, mine):
    square = jnp.full((BLK, BLK), core_square, f32)
    for a in range(3):
        diff = theirs[:, a : a + 1] - mine[a : a + 1, :]
        square = square + diff * diff
    dist = jnp.sqrt(square)
    x = dist * (1.0 / time_step)
    term = jnp.exp(-x) * (SCALE / (4.0 * math.pi)) / dist
    hi, low = split(term * jnp.exp(-damping * x))
    sample[p, :, :BLK] = hi
    sample[p, :, BLK:] = low.astype(bf16)
    for n in range(TAIL):
        side, place = divmod(n, HALF)
        hi, low = split(term)
        main[p, place * BLK : (place + 1) * BLK, side * BLK : (side + 1) * BLK] = hi
        if n < 2 * CORR:
            side, place = divmod(n, CORR)
            first = (place // 2 * 4 + place % 2) * BLK
            lanes = slice(side * BLK, (side + 1) * BLK)
            fine[p, first : first + BLK, lanes] = (low * TERM_UP).astype(fp8)
            fine[p, first + 2 * BLK : first + 3 * BLK, lanes] = term.astype(fp8)
        if n + 1 < TAIL:
            term = term * (x * (1.0 / (n + 1)))


def contract(pair_data, four_data, main, fine, wide, narrow, p, c, first, last):
    rows = last - first
    total = None
    for k in range(HALF // 2):
        start = HEAD - LEAD + first - 2 * k
        term = product(pair_data[c, start : start + rows, :], main[p, k * WIDE : (k + 1) * WIDE, :])
        total = term if total is None else total + term
    wide[p, first:last, :] = total
    total = None
    for k in range(0, CORR, 4):
        start = HEAD - LEAD + first - k
        depth = 2 * min(4, CORR - k) * BLK
        term = product(
            four_data[c, start : start + rows, :depth], fine[p, 2 * k * BLK : 2 * k * BLK + depth, :]
        )
        total = term if total is None else total + term
    narrow[p, first:last, :] = total


def gather(wide, narrow, p, first, last):
    a, b = LEAD + first, LEAD + last
    low = narrow[p, a:b, :BLK] + narrow[p, a - CORR : b - CORR, BLK:]
    high = wide[p, a:b, :BLK] + wide[p, a - HALF : b - HALF, BLK:]
    return high * (1.0 / SCALE) + low * (1.0 / (SCALE * FIELD_UP * TERM_UP))


def operator(
    list_hbm,
    count_hbm,
    traces_ref,
    xyz_hbm,
    out_ref,
    ext,
    head,
    slots,
    mark,
    parts,
    corner,
    sums,
    xyz_ref,
    list_ref,
    count_ref,
    pair_data,
    four_data,
    main,
    fine,
    sample,
    wide,
    narrow,
    turned,
    shape,
    send,
    recv,
    load,
    ready,
):
    steps, width = traces_ref.shape
    blocks = width // BLK
    geo = START + steps
    groups = lax.axis_size("freq")
    shards = lax.axis_size("panel")
    position = lax.axis_index("freq")
    shard = lax.axis_index("panel")
    pairs = list_ref.shape[1]
    rows = steps + LEAD

    def device(ahead, side):
        return {
            "freq": lax.rem(position + ahead + groups, groups),
            "panel": lax.rem(shard + side + shards, shards),
        }

    def signal(semaphore, ahead, side):
        pl.semaphore_signal(
            semaphore,
            inc=1,
            device_id=device(ahead, side),
            device_id_type=pl.DeviceIdType.MESH,
        )

    barrier = pltpu.get_barrier_semaphore()
    signal(barrier, 0, 1)
    signal(barrier, 0, -1)
    sides = (0, 1, -1)
    for s in range(1, groups):

        @pl.when(position + s < groups)
        def _():
            for d in sides:
                signal(barrier, s, d)

    loads = [pltpu.make_async_copy(xyz_hbm, xyz_ref, load.at[blocks])]
    loads += [
        pltpu.make_async_copy(
            traces_ref.at[:, pl.ds(b * BLK, BLK)],
            ext.at[b + 1, pl.ds(START, steps)],
            load.at[b],
        )
        for b in range(blocks)
    ]
    loads.append(pltpu.make_async_copy(list_hbm, list_ref, load.at[blocks + 1]))
    loads.append(pltpu.make_async_copy(count_hbm, count_ref, load.at[blocks + 2]))
    for copy in loads:
        copy.start()

    made = []

    def remote(ahead, side, source, target):
        i = len(made)
        made.append(i)
        return pltpu.make_async_remote_copy(
            src_ref=source,
            dst_ref=target,
            send_sem=send.at[i],
            recv_sem=recv.at[i],
            device_id=device(ahead, side),
            device_id_type=pl.DeviceIdType.MESH,
        )

    own = pl.ds(START, steps)
    tail = pl.ds(steps - TAIL, TAIL)
    left, right = pl.ds(0, BLK), pl.ds((blocks - 1) * BLK, BLK)
    edges = [
        remote(0, 1, traces_ref.at[:, right], ext.at[0, own]),
        remote(0, -1, traces_ref.at[:, left], ext.at[blocks + 1, own]),
    ]
    marks = [
        remote(0, 1, mark.at[blocks - 1], shape.at[0]),
        remote(0, -1, mark.at[0], shape.at[blocks + 1]),
    ]
    tails = [
        remote(1, 0, traces_ref.at[tail, :], head),
        remote(1, 1, traces_ref.at[tail, right], corner.at[0]),
        remote(1, -1, traces_ref.at[tail, left], corner.at[1]),
    ]
    nears = [remote(0, 1, parts, slots.at[0, 1]), remote(0, -1, parts, slots.at[0, 2])]
    turns = [
        [remote(s, d, parts, slots.at[s, n]) for n, d in enumerate(sides)] for s in range(1, groups)
    ]

    times = position * steps + lax.broadcasted_iota(jnp.int32, (steps, BLK), 0)
    weight = jnp.exp(times.astype(f32) * math.log(damping))
    weight = jnp.where(times % 2 == 0, weight, -weight)

    loads[0].wait()
    for b in range(blocks):
        mark[b, 0:3, :] = xyz_ref[:, b * BLK : (b + 1) * BLK]
        mark[b, 3:, :] = jnp.zeros((GEO - 3, BLK), f32)
    pl.semaphore_wait(barrier, 2 + len(sides) * position)
    for copy in marks:
        copy.start()
    for s in range(1, groups):

        @pl.when(position >= s)
        def _():
            signal(ready.at[s], -s, 0)

    @pl.when(position + 1 >= groups)
    def _():
        for copy in tails:
            copy.start()

    for copy in edges:
        copy.start()
    for copy in loads[1:]:
        copy.wait()
    parts[blocks:, :] = jnp.zeros((GEO - blocks, BLK), f32)
    for b in range(blocks):
        parts[b : b + 1, :] = jnp.sum(weight * ext[b + 1, START:geo, :], axis=0, keepdims=True)
    for copy in nears:
        copy.start()
    for s in range(1, groups):

        @pl.when(position + s >= groups)
        def _():
            for copy in turns[s - 1]:
                copy.start()

    def up(s):
        @pl.when(position + s < groups)
        def _():
            pl.semaphore_wait(ready.at[s], 1)
            for copy in (tails if s == 1 else []) + turns[s - 1]:
                copy.start()

    ext[:, :START, :] = jnp.zeros((blocks + 2, START, BLK), f32)
    for c in range(1, blocks + 1):
        spread(ext, pair_data, four_data, c, HEAD, steps)
        shape[c] = mark[c - 1]
        turned[c] = turn(shape[c])
    fixed = [(n, n + 1) for n in range(blocks)] + [(0, 0), (blocks - 1, blocks + 1)]
    for p, (r, c) in enumerate(fixed[:blocks]):
        fill(main, fine, sample, p, turned[c], shape[r + 1])
        contract(pair_data, four_data, main, fine, wide, narrow, p, c, HEAD, rows)
        if p == 0:
            up(1)

    for copy in marks:
        copy.wait()
    for c in (0, blocks + 1):
        turned[c] = turn(shape[c])
    order = list(fixed)
    order += [(list_ref[0, p], list_ref[1, p]) for p in range(len(fixed), pairs)]
    for p in range(blocks, pairs):
        r, c = order[p]
        fill(main, fine, sample, p, turned[c], shape[r + 1])

    for copy in edges:
        copy.wait()
    for n, c in enumerate((0, blocks + 1)):
        spread(ext, pair_data, four_data, c, HEAD, steps)
        contract(pair_data, four_data, main, fine, wide, narrow, blocks + n, c, HEAD, rows)
    for p in range(len(fixed), pairs):
        contract(pair_data, four_data, main, fine, wide, narrow, p, order[p][1], HEAD, rows)
    for s in range(2, groups):
        up(s)

    def collect(first, last):
        for r in range(blocks):
            total = None
            for p, (row, _) in enumerate(fixed):
                if row == r:
                    term = gather(wide, narrow, p, first, last)
                    total = term if total is None else total + term
            out_ref[first:last, r * BLK : (r + 1) * BLK] = total
        for p in range(len(fixed), pairs):
            total = gather(wide, narrow, p, first, last)
            for r in range(blocks):
                lanes = slice(r * BLK, (r + 1) * BLK)
                out_ref[first:last, lanes] = out_ref[first:last, lanes] + jnp.where(
                    targets[p] == r, total, 0.0
                )

    targets = {
        p: jnp.where(p < count_ref[0], order[p][0], blocks) for p in range(len(fixed), pairs)
    }
    around = jnp.where(position == 0, math.exp(NT * math.log(damping)), 1.0)
    local = lax.broadcasted_iota(jnp.int32, (steps, BLK), 0)
    growth = jnp.exp((position * steps + local).astype(f32) * -math.log(damping)) / (NT * SCALE)
    growth = jnp.where(local % 2 == 0, -growth, growth)
    pick = lax.broadcasted_iota(jnp.int32, (2 * GEO, BLK), 0)

    def follow(c, before):
        ext[c, START - TAIL : START, :] = before * around
        spread(ext, pair_data, four_data, c, 0, HEAD + LEAD)

    for copy in tails:
        copy.wait()
    for c in range(1, blocks + 1):
        follow(c, head[:, (c - 1) * BLK : c * BLK])
    follow(0, corner[0])
    follow(blocks + 1, corner[1])
    if steps > HEAD:
        collect(HEAD, steps)
    for p in range(blocks):
        contract(pair_data, four_data, main, fine, wide, narrow, p, p + 1, 0, HEAD)
    contract(pair_data, four_data, main, fine, wide, narrow, blocks, 0, 0, HEAD)
    contract(pair_data, four_data, main, fine, wide, narrow, blocks + 1, blocks + 1, 0, HEAD)
    for p in range(len(fixed), pairs):
        contract(pair_data, four_data, main, fine, wide, narrow, p, order[p][1], 0, HEAD)

    for some in [nears] + turns:
        for copy in some:
            copy.wait()
    for c in range(blocks + 2):
        n, b = (1, blocks - 1) if c == 0 else (2, 0) if c > blocks else (0, c - 1)
        total = parts[b : b + 1, :] if n == 0 else slots[0, n, b : b + 1, :]
        for s in range(1, groups):
            total = total + slots[s, n, b : b + 1, :]
        total = jnp.broadcast_to(total, (2 * GEO, BLK))
        hi, low = split(total)
        sums[c] = jnp.where(pick == 0, total, jnp.where(pick == 1, low, 0.0)).astype(bf16)

    ranks = []
    for p in range(pairs):
        both = product(sums[order[p][1]], sample[p])
        ranks.append(both[0:1, :BLK] + (both[1:2, :BLK] + both[0:1, BLK:]))
    collect(0, HEAD)
    for r in range(blocks):
        rank = jnp.zeros((1, BLK), f32)
        for p in range(pairs):
            if p < len(fixed):
                rank = rank + ranks[p] if fixed[p][0] == r else rank
            else:
                rank = rank + jnp.where(targets[p] == r, ranks[p], 0.0)
        lanes = slice(r * BLK, (r + 1) * BLK)
        out_ref[:, lanes] = out_ref[:, lanes] + growth * rank


def per_device(traces, centroids, near_list, pair_count):
    steps, width = traces.shape
    blocks = width // BLK
    pairs = near_list.shape[1]
    groups = lax.axis_size("freq")
    count = 6 + 3 * groups
    hbm = pl.BlockSpec(memory_space=pltpu.HBM)
    given = [pltpu.with_memory_space_constraint(v, pltpu.HBM) for v in (traces, centroids)]
    return pl.pallas_call(
        operator,
        out_shape=pltpu.VMEM((steps, width), f32),
        in_specs=[hbm] * 4,
        out_specs=pl.BlockSpec(memory_space=pltpu.VMEM),
        scratch_shapes=[
            pltpu.VMEM((blocks + 2, START + steps, BLK), f32),
            pltpu.VMEM((TAIL, width), f32),
            pltpu.VMEM((groups, 3, GEO, BLK), f32),
            pltpu.VMEM((blocks, GEO, BLK), f32),
            pltpu.VMEM((GEO, BLK), f32),
            pltpu.VMEM((2, TAIL, BLK), f32),
            pltpu.VMEM((blocks + 2, 2 * GEO, BLK), bf16),
            pltpu.VMEM((3, width), f32),
            pltpu.SMEM((2, pairs), jnp.int32),
            pltpu.SMEM((1,), jnp.int32),
            pltpu.VMEM((blocks + 2, HEAD + steps, WIDE), bf16),
            pltpu.VMEM((blocks + 2, HEAD + steps, 8 * BLK), fp8),
            pltpu.VMEM((pairs, HALF * BLK, WIDE), bf16),
            pltpu.VMEM((pairs, 2 * CORR * BLK, WIDE), fp8),
            pltpu.VMEM((pairs, BLK, WIDE), bf16),
            pltpu.VMEM((pairs, LEAD + steps, WIDE), f32),
            pltpu.VMEM((pairs, LEAD + steps, WIDE), f32),
            pltpu.VMEM((blocks + 2, BLK, BLK), f32),
            pltpu.VMEM((blocks + 2, GEO, BLK), f32),
            pltpu.SemaphoreType.DMA((count,)),
            pltpu.SemaphoreType.DMA((count,)),
            pltpu.SemaphoreType.DMA((blocks + 3,)),
            pltpu.SemaphoreType.REGULAR((groups,)),
        ],
        compiler_params=pltpu.CompilerParams(
            collective_id=0, has_side_effects=True, vmem_limit_bytes=60 * 1024 * 1024
        ),
    )(near_list[0].T, pair_count, *given)


def solution(mesh):
    in_specs = (
        P("freq", ("grp", "panel")),
        P(None, ("grp", "panel")),
        P(("grp", "panel"), None, None),
        P(("grp", "panel")),
    )
    out_specs = P("freq", ("grp", "panel"))
    return jax.shard_map(
        per_device, mesh=mesh, in_specs=in_specs, out_specs=out_specs, check_vma=False
    )
```

```python
import math

import jax
import jax.numpy as jnp
from jax import lax
from jax.experimental import pallas as pl
from jax.experimental.pallas import tpu as pltpu
from jax.sharding import PartitionSpec as P

NT = 1024
BLK = 128
GEO = 8
TAIL = 24
HEAD = 32
PAD = 8
START = PAD + HEAD
LEAD = 16
HALF = 12
CORR = 6
FIXED = 5
WIDE = 2 * BLK

SCALE = 512.0
FIELD_UP = 32.0
LOW_UP = 8192.0
TERM_UP = 256.0

damping = 0.999
time_step = 0.5
core_square = 0.01

bf16 = jnp.bfloat16
fp8 = jnp.float8_e4m3fn
f32 = jnp.float32


def product(x, y):
    return jnp.dot(x, y, preferred_element_type=f32)


def split(v):
    hi = v.astype(bf16)
    return hi, v - hi.astype(f32)


def turn(geometry):
    return jnp.concatenate([geometry] * (BLK // GEO), axis=0).T


def spread(ext, pair_data, four_data, c, first, rows):
    for n in range(4):
        v = ext[c, PAD + first - n : PAD + first - n + rows, :]
        hi, low = split(v)
        if n < 2:
            pair_data[c, first : first + rows, n * BLK : (n + 1) * BLK] = hi
        at = (n // 2 * 4 + n % 2) * BLK
        four_data[c, first : first + rows, at : at + BLK] = (v * FIELD_UP).astype(fp8)
        at = at + 2 * BLK
        four_data[c, first : first + rows, at : at + BLK] = (low * LOW_UP).astype(fp8)


def fill(main, fine, sample, p, theirs, mine):
    square = jnp.full((BLK, BLK), core_square, f32)
    for a in range(3):
        diff = theirs[:, a : a + 1] - mine[a : a + 1, :]
        square = square + diff * diff
    dist = jnp.sqrt(square)
    x = dist * (1.0 / time_step)
    term = jnp.exp(-x) * (SCALE / (4.0 * math.pi)) / dist
    hi, low = split(term * jnp.exp(-damping * x))
    sample[p, :, :BLK] = hi
    sample[p, :, BLK:] = low.astype(bf16)
    for n in range(TAIL):
        side, place = divmod(n, HALF)
        hi, low = split(term)
        main[p, place * BLK : (place + 1) * BLK, side * BLK : (side + 1) * BLK] = hi
        if n < 2 * CORR:
            side, place = divmod(n, CORR)
            first = (place // 2 * 4 + place % 2) * BLK
            lanes = slice(side * BLK, (side + 1) * BLK)
            fine[p, first : first + BLK, lanes] = (low * TERM_UP).astype(fp8)
            fine[p, first + 2 * BLK : first + 3 * BLK, lanes] = term.astype(fp8)
        if n + 1 < TAIL:
            term = term * (x * (1.0 / (n + 1)))


def contract(pair_data, four_data, main, fine, wide, narrow, p, c, first, last):
    rows = last - first
    total = None
    for k in range(HALF // 2):
        start = HEAD - LEAD + first - 2 * k
        term = product(pair_data[c, start : start + rows, :], main[p, k * WIDE : (k + 1) * WIDE, :])
        total = term if total is None else total + term
    wide[p, first:last, :] = total
    total = None
    for k in range(0, CORR, 4):
        start = HEAD - LEAD + first - k
        depth = 2 * min(4, CORR - k) * BLK
        term = product(
            four_data[c, start : start + rows, :depth], fine[p, 2 * k * BLK : 2 * k * BLK + depth, :]
        )
        total = term if total is None else total + term
    narrow[p, first:last, :] = total


def gather(wide, narrow, p, first, last):
    a, b = LEAD + first, LEAD + last
    low = narrow[p, a:b, :BLK] + narrow[p, a - CORR : b - CORR, BLK:]
    high = wide[p, a:b, :BLK] + wide[p, a - HALF : b - HALF, BLK:]
    return high * (1.0 / SCALE) + low * (1.0 / (SCALE * FIELD_UP * TERM_UP))


def operator(
    list_hbm,
    count_hbm,
    traces_ref,
    xyz_hbm,
    out_ref,
    ext,
    head,
    slots,
    mark,
    parts,
    corner,
    sums,
    xyz_ref,
    list_ref,
    count_ref,
    pair_data,
    four_data,
    main,
    fine,
    sample,
    wide,
    narrow,
    turned,
    shape,
    send,
    recv,
    load,
    ready,
):
    steps, width = traces_ref.shape
    blocks = width // BLK
    geo = START + steps
    groups = lax.axis_size("freq")
    shards = lax.axis_size("panel")
    position = lax.axis_index("freq")
    shard = lax.axis_index("panel")
    pairs = list_ref.shape[1]
    rows = steps + LEAD

    def device(ahead, side):
        return {
            "freq": lax.rem(position + ahead + groups, groups),
            "panel": lax.rem(shard + side + shards, shards),
        }

    def signal(semaphore, ahead, side):
        pl.semaphore_signal(
            semaphore,
            inc=1,
            device_id=device(ahead, side),
            device_id_type=pl.DeviceIdType.MESH,
        )

    loads = [pltpu.make_async_copy(xyz_hbm, xyz_ref, load.at[blocks])]
    loads += [
        pltpu.make_async_copy(
            traces_ref.at[:, pl.ds(b * BLK, BLK)],
            ext.at[b + 1, pl.ds(START, steps)],
            load.at[b],
        )
        for b in range(blocks)
    ]
    loads.append(pltpu.make_async_copy(list_hbm, list_ref, load.at[blocks + 1]))
    loads.append(pltpu.make_async_copy(count_hbm, count_ref, load.at[blocks + 2]))
    for copy in loads:
        copy.start()

    barrier = pltpu.get_barrier_semaphore()
    signal(barrier, 0, 1)
    signal(barrier, 0, -1)
    sides = (0, 1, -1)
    for s in range(1, groups):

        @pl.when(position + s < groups)
        def _():
            for d in sides:
                signal(barrier, s, d)

    made = []

    def remote(ahead, side, source, target):
        i = len(made)
        made.append(i)
        return pltpu.make_async_remote_copy(
            src_ref=source,
            dst_ref=target,
            send_sem=send.at[i],
            recv_sem=recv.at[i],
            device_id=device(ahead, side),
            device_id_type=pl.DeviceIdType.MESH,
        )

    own = pl.ds(START, steps)
    tail = pl.ds(steps - TAIL, TAIL)
    left, right = pl.ds(0, BLK), pl.ds((blocks - 1) * BLK, BLK)
    edges = [
        remote(0, 1, traces_ref.at[:, right], ext.at[0, own]),
        remote(0, -1, traces_ref.at[:, left], ext.at[blocks + 1, own]),
    ]
    marks = [
        remote(0, 1, mark.at[blocks - 1], shape.at[0]),
        remote(0, -1, mark.at[0], shape.at[blocks + 1]),
    ]
    tails = [
        remote(1, 0, traces_ref.at[tail, :], head),
        remote(1, 1, traces_ref.at[tail, right], corner.at[0]),
        remote(1, -1, traces_ref.at[tail, left], corner.at[1]),
    ]
    nears = [remote(0, 1, parts, slots.at[0, 1]), remote(0, -1, parts, slots.at[0, 2])]
    turns = [
        [remote(s, d, parts, slots.at[s, n]) for n, d in enumerate(sides)] for s in range(1, groups)
    ]

    times = position * steps + lax.broadcasted_iota(jnp.int32, (steps, BLK), 0)
    weight = jnp.exp(times.astype(f32) * math.log(damping))
    weight = jnp.where(times % 2 == 0, weight, -weight)

    loads[0].wait()
    for b in range(blocks):
        mark[b, 0:3, :] = xyz_ref[:, b * BLK : (b + 1) * BLK]
        mark[b, 3:, :] = jnp.zeros((GEO - 3, BLK), f32)
    pl.semaphore_wait(barrier, 2 + len(sides) * position)
    for copy in marks:
        copy.start()
    for s in range(1, groups):

        @pl.when(position >= s)
        def _():
            signal(ready.at[s], -s, 0)

    @pl.when(position + 1 >= groups)
    def _():
        for copy in tails:
            copy.start()

    for copy in edges:
        copy.start()
    for copy in loads[1:]:
        copy.wait()
    parts[blocks:, :] = jnp.zeros((GEO - blocks, BLK), f32)
    for b in range(blocks):
        parts[b : b + 1, :] = jnp.sum(weight * ext[b + 1, START:geo, :], axis=0, keepdims=True)
    for copy in nears:
        copy.start()
    for s in range(1, groups):

        @pl.when(position + s >= groups)
        def _():
            for copy in turns[s - 1]:
                copy.start()

    def up(s):
        @pl.when(position + s < groups)
        def _():
            pl.semaphore_wait(ready.at[s], 1)
            for copy in (tails if s == 1 else []) + turns[s - 1]:
                copy.start()

    ext[:, :START, :] = jnp.zeros((blocks + 2, START, BLK), f32)
    for c in range(1, blocks + 1):
        spread(ext, pair_data, four_data, c, HEAD, steps)
        shape[c] = mark[c - 1]
        turned[c] = turn(shape[c])
    fixed = [(n, n + 1) for n in range(blocks)] + [(0, 0), (blocks - 1, blocks + 1)]
    for p, (r, c) in enumerate(fixed[:blocks]):
        fill(main, fine, sample, p, turned[c], shape[r + 1])
        contract(pair_data, four_data, main, fine, wide, narrow, p, c, HEAD, rows)
        if p == 0:
            up(1)

    for copy in marks:
        copy.wait()
    for c in (0, blocks + 1):
        turned[c] = turn(shape[c])
    order = list(fixed)
    order += [(list_ref[0, p], list_ref[1, p]) for p in range(len(fixed), pairs)]
    for p in range(blocks, pairs):
        r, c = order[p]
        fill(main, fine, sample, p, turned[c], shape[r + 1])

    for copy in edges:
        copy.wait()
    for n, c in enumerate((0, blocks + 1)):
        spread(ext, pair_data, four_data, c, HEAD, steps)
        contract(pair_data, four_data, main, fine, wide, narrow, blocks + n, c, HEAD, rows)
    contract(pair_data, four_data, main, fine, wide, narrow, len(fixed), order[len(fixed)][1], HEAD, rows)
    for s in range(2, groups):
        up(s)

    def collect(first, last):
        for r in range(blocks):
            total = None
            for p, (row, _) in enumerate(fixed):
                if row == r:
                    term = gather(wide, narrow, p, first, last)
                    total = term if total is None else total + term
            out_ref[first:last, r * BLK : (r + 1) * BLK] = total
        for p in range(len(fixed), pairs):
            total = gather(wide, narrow, p, first, last)
            for r in range(blocks):
                lanes = slice(r * BLK, (r + 1) * BLK)
                out_ref[first:last, lanes] = out_ref[first:last, lanes] + jnp.where(
                    targets[p] == r, total, 0.0
                )

    targets = {
        p: jnp.where(p < count_ref[0], order[p][0], blocks) for p in range(len(fixed), pairs)
    }
    around = jnp.where(position == 0, math.exp(NT * math.log(damping)), 1.0)
    local = lax.broadcasted_iota(jnp.int32, (steps, BLK), 0)
    growth = jnp.exp((position * steps + local).astype(f32) * -math.log(damping)) / (NT * SCALE)
    growth = jnp.where(local % 2 == 0, -growth, growth)
    pick = lax.broadcasted_iota(jnp.int32, (2 * GEO, BLK), 0)

    def follow(c, before):
        ext[c, START - TAIL : START, :] = before * around
        spread(ext, pair_data, four_data, c, 0, HEAD + LEAD)

    for copy in tails:
        copy.wait()
    for c in range(1, blocks + 1):
        follow(c, head[:, (c - 1) * BLK : c * BLK])
    follow(0, corner[0])
    follow(blocks + 1, corner[1])
    for p in range(blocks):
        contract(pair_data, four_data, main, fine, wide, narrow, p, p + 1, 0, HEAD)
    contract(pair_data, four_data, main, fine, wide, narrow, blocks, 0, 0, HEAD)
    contract(pair_data, four_data, main, fine, wide, narrow, blocks + 1, blocks + 1, 0, HEAD)
    for p in range(len(fixed), pairs):
        contract(pair_data, four_data, main, fine, wide, narrow, p, order[p][1], 0, HEAD if p == len(fixed) else rows)

    if steps > HEAD:
        collect(HEAD, steps)
    collect(0, HEAD)
    for some in [nears] + turns:
        for copy in some:
            copy.wait()
    for c in range(blocks + 2):
        n, b = (1, blocks - 1) if c == 0 else (2, 0) if c > blocks else (0, c - 1)
        total = parts[b : b + 1, :] if n == 0 else slots[0, n, b : b + 1, :]
        for s in range(1, groups):
            total = total + slots[s, n, b : b + 1, :]
        total = jnp.broadcast_to(total, (2 * GEO, BLK))
        hi, low = split(total)
        sums[c] = jnp.where(pick == 0, total, jnp.where(pick == 1, low, 0.0)).astype(bf16)

    ranks = []
    for p in range(pairs):
        both = product(sums[order[p][1]], sample[p])
        ranks.append(both[0:1, :BLK] + (both[1:2, :BLK] + both[0:1, BLK:]))
    for r in range(blocks):
        rank = jnp.zeros((1, BLK), f32)
        for p in range(pairs):
            if p < len(fixed):
                rank = rank + ranks[p] if fixed[p][0] == r else rank
            else:
                rank = rank + jnp.where(targets[p] == r, ranks[p], 0.0)
        lanes = slice(r * BLK, (r + 1) * BLK)
        out_ref[:, lanes] = out_ref[:, lanes] + growth * rank


def per_device(traces, centroids, near_list, pair_count):
    steps, width = traces.shape
    blocks = width // BLK
    pairs = near_list.shape[1]
    groups = lax.axis_size("freq")
    count = 6 + 3 * groups
    hbm = pl.BlockSpec(memory_space=pltpu.HBM)
    given = [pltpu.with_memory_space_constraint(v, pltpu.HBM) for v in (traces, centroids)]
    return pl.pallas_call(
        operator,
        out_shape=pltpu.VMEM((steps, width), f32),
        in_specs=[hbm] * 4,
        out_specs=pl.BlockSpec(memory_space=pltpu.VMEM),
        scratch_shapes=[
            pltpu.VMEM((blocks + 2, START + steps, BLK), f32),
            pltpu.VMEM((TAIL, width), f32),
            pltpu.VMEM((groups, 3, GEO, BLK), f32),
            pltpu.VMEM((blocks, GEO, BLK), f32),
            pltpu.VMEM((GEO, BLK), f32),
            pltpu.VMEM((2, TAIL, BLK), f32),
            pltpu.VMEM((blocks + 2, 2 * GEO, BLK), bf16),
            pltpu.VMEM((3, width), f32),
            pltpu.SMEM((2, pairs), jnp.int32),
            pltpu.SMEM((1,), jnp.int32),
            pltpu.VMEM((blocks + 2, HEAD + steps, WIDE), bf16),
            pltpu.VMEM((blocks + 2, HEAD + steps, 8 * BLK), fp8),
            pltpu.VMEM((pairs, HALF * BLK, WIDE), bf16),
            pltpu.VMEM((pairs, 2 * CORR * BLK, WIDE), fp8),
            pltpu.VMEM((pairs, BLK, WIDE), bf16),
            pltpu.VMEM((pairs, LEAD + steps, WIDE), f32),
            pltpu.VMEM((pairs, LEAD + steps, WIDE), f32),
            pltpu.VMEM((blocks + 2, BLK, BLK), f32),
            pltpu.VMEM((blocks + 2, GEO, BLK), f32),
            pltpu.SemaphoreType.DMA((count,)),
            pltpu.SemaphoreType.DMA((count,)),
            pltpu.SemaphoreType.DMA((blocks + 3,)),
            pltpu.SemaphoreType.REGULAR((groups,)),
        ],
        compiler_params=pltpu.CompilerParams(
            collective_id=0, has_side_effects=True, vmem_limit_bytes=60 * 1024 * 1024
        ),
    )(near_list[0].T, pair_count, *given)


def solution(mesh):
    in_specs = (
        P("freq", ("grp", "panel")),
        P(None, ("grp", "panel")),
        P(("grp", "panel"), None, None),
        P(("grp", "panel")),
    )
    out_specs = P("freq", ("grp", "panel"))
    return jax.shard_map(
        per_device, mesh=mesh, in_specs=in_specs, out_specs=out_specs, check_vma=False
    )
```

```python
import math

import jax
import jax.numpy as jnp
from jax import lax
from jax.experimental import pallas as pl
from jax.experimental.pallas import tpu as pltpu
from jax.sharding import PartitionSpec as P

NT = 1024
BLK = 128
GEO = 8
TAIL = 24
HEAD = 32
PAD = 8
START = PAD + HEAD
LEAD = 16
HALF = 12
CORR = 6
FIXED = 5
WIDE = 2 * BLK

SCALE = 512.0
FIELD_UP = 32.0
LOW_UP = 8192.0
TERM_UP = 256.0

damping = 0.999
time_step = 0.5
core_square = 0.01

bf16 = jnp.bfloat16
fp8 = jnp.float8_e4m3fn
f32 = jnp.float32


def product(x, y):
    return jnp.dot(x, y, preferred_element_type=f32)


def split(v):
    hi = v.astype(bf16)
    return hi, v - hi.astype(f32)


def turn(geometry):
    return jnp.concatenate([geometry] * (BLK // GEO), axis=0).T


def spread(ext, pair_data, four_data, c, first, rows):
    for n in range(4):
        v = ext[c, PAD + first - n : PAD + first - n + rows, :]
        hi, low = split(v)
        if n < 2:
            pair_data[c, first : first + rows, n * BLK : (n + 1) * BLK] = hi
        at = (n // 2 * 4 + n % 2) * BLK
        four_data[c, first : first + rows, at : at + BLK] = (v * FIELD_UP).astype(fp8)
        at = at + 2 * BLK
        four_data[c, first : first + rows, at : at + BLK] = (low * LOW_UP).astype(fp8)


def fill(main, fine, sample, p, theirs, mine):
    square = jnp.full((BLK, BLK), core_square, f32)
    for a in range(3):
        diff = theirs[:, a : a + 1] - mine[a : a + 1, :]
        square = square + diff * diff
    dist = jnp.sqrt(square)
    x = dist * (1.0 / time_step)
    term = jnp.exp(-x) * (SCALE / (4.0 * math.pi)) / dist
    hi, low = split(term * jnp.exp(-damping * x))
    sample[p, :, :BLK] = hi
    sample[p, :, BLK:] = low.astype(bf16)
    for n in range(TAIL):
        side, place = divmod(n, HALF)
        hi, low = split(term)
        main[p, place * BLK : (place + 1) * BLK, side * BLK : (side + 1) * BLK] = hi
        if n < 2 * CORR:
            side, place = divmod(n, CORR)
            first = (place // 2 * 4 + place % 2) * BLK
            lanes = slice(side * BLK, (side + 1) * BLK)
            fine[p, first : first + BLK, lanes] = (low * TERM_UP).astype(fp8)
            fine[p, first + 2 * BLK : first + 3 * BLK, lanes] = term.astype(fp8)
        if n + 1 < TAIL:
            term = term * (x * (1.0 / (n + 1)))


def contract(pair_data, four_data, main, fine, wide, narrow, p, c, first, last):
    rows = last - first
    total = None
    for k in range(HALF // 2):
        start = HEAD - LEAD + first - 2 * k
        term = product(pair_data[c, start : start + rows, :], main[p, k * WIDE : (k + 1) * WIDE, :])
        total = term if total is None else total + term
    wide[p, first:last, :] = total
    total = None
    for k in range(0, CORR, 4):
        start = HEAD - LEAD + first - k
        depth = 2 * min(4, CORR - k) * BLK
        term = product(
            four_data[c, start : start + rows, :depth], fine[p, 2 * k * BLK : 2 * k * BLK + depth, :]
        )
        total = term if total is None else total + term
    narrow[p, first:last, :] = total


def gather(wide, narrow, p, first, last):
    a, b = LEAD + first, LEAD + last
    low = narrow[p, a:b, :BLK] + narrow[p, a - CORR : b - CORR, BLK:]
    high = wide[p, a:b, :BLK] + wide[p, a - HALF : b - HALF, BLK:]
    return high * (1.0 / SCALE) + low * (1.0 / (SCALE * FIELD_UP * TERM_UP))


def operator(
    list_hbm,
    count_hbm,
    traces_ref,
    xyz_hbm,
    out_ref,
    ext,
    head,
    slots,
    mark,
    parts,
    corner,
    sums,
    xyz_ref,
    list_ref,
    count_ref,
    pair_data,
    four_data,
    main,
    fine,
    sample,
    wide,
    narrow,
    turned,
    shape,
    send,
    recv,
    load,
    ready,
):
    steps, width = traces_ref.shape
    blocks = width // BLK
    geo = START + steps
    groups = lax.axis_size("freq")
    shards = lax.axis_size("panel")
    position = lax.axis_index("freq")
    shard = lax.axis_index("panel")
    pairs = list_ref.shape[1]
    rows = steps + LEAD

    def device(ahead, side):
        return {
            "freq": lax.rem(position + ahead + groups, groups),
            "panel": lax.rem(shard + side + shards, shards),
        }

    def signal(semaphore, ahead, side):
        pl.semaphore_signal(
            semaphore,
            inc=1,
            device_id=device(ahead, side),
            device_id_type=pl.DeviceIdType.MESH,
        )

    loads = [pltpu.make_async_copy(xyz_hbm, xyz_ref, load.at[blocks])]
    loads += [
        pltpu.make_async_copy(
            traces_ref.at[:, pl.ds(b * BLK, BLK)],
            ext.at[b + 1, pl.ds(START, steps)],
            load.at[b],
        )
        for b in range(blocks)
    ]
    loads.append(pltpu.make_async_copy(list_hbm, list_ref, load.at[blocks + 1]))
    loads.append(pltpu.make_async_copy(count_hbm, count_ref, load.at[blocks + 2]))
    for copy in loads:
        copy.start()

    barrier = pltpu.get_barrier_semaphore()
    signal(barrier, 0, 1)
    signal(barrier, 0, -1)
    sides = (0, 1, -1)
    for s in range(1, groups):

        @pl.when(position + s < groups)
        def _():
            for d in sides:
                signal(barrier, s, d)

    made = []

    def remote(ahead, side, source, target):
        i = len(made)
        made.append(i)
        return pltpu.make_async_remote_copy(
            src_ref=source,
            dst_ref=target,
            send_sem=send.at[i],
            recv_sem=recv.at[i],
            device_id=device(ahead, side),
            device_id_type=pl.DeviceIdType.MESH,
        )

    own = pl.ds(START, steps)
    tail = pl.ds(steps - TAIL, TAIL)
    left, right = pl.ds(0, BLK), pl.ds((blocks - 1) * BLK, BLK)
    edges = [
        remote(0, 1, traces_ref.at[:, right], ext.at[0, own]),
        remote(0, -1, traces_ref.at[:, left], ext.at[blocks + 1, own]),
    ]
    marks = [
        remote(0, 1, mark.at[blocks - 1], shape.at[0]),
        remote(0, -1, mark.at[0], shape.at[blocks + 1]),
    ]
    tails = [
        remote(1, 0, traces_ref.at[tail, :], head),
        remote(1, 1, traces_ref.at[tail, right], corner.at[0]),
        remote(1, -1, traces_ref.at[tail, left], corner.at[1]),
    ]
    nears = [remote(0, 1, parts, slots.at[0, 1]), remote(0, -1, parts, slots.at[0, 2])]
    turns = [
        [remote(s, d, parts, slots.at[s, n]) for n, d in enumerate(sides)] for s in range(1, groups)
    ]

    times = position * steps + lax.broadcasted_iota(jnp.int32, (steps, BLK), 0)
    weight = jnp.exp(times.astype(f32) * math.log(damping))
    weight = jnp.where(times % 2 == 0, weight, -weight)

    loads[0].wait()
    for b in range(blocks):
        mark[b, 0:3, :] = xyz_ref[:, b * BLK : (b + 1) * BLK]
        mark[b, 3:, :] = jnp.zeros((GEO - 3, BLK), f32)
    pl.semaphore_wait(barrier, 2 + len(sides) * position)
    for copy in marks:
        copy.start()
    for s in range(1, groups):

        @pl.when(position >= s)
        def _():
            signal(ready.at[s], -s, 0)

    @pl.when(position + 1 >= groups)
    def _():
        for copy in tails:
            copy.start()

    for copy in edges:
        copy.start()
    for copy in loads[1:]:
        copy.wait()
    parts[blocks:, :] = jnp.zeros((GEO - blocks, BLK), f32)
    for b in range(blocks):
        parts[b : b + 1, :] = jnp.sum(weight * ext[b + 1, START:geo, :], axis=0, keepdims=True)
    for copy in nears:
        copy.start()
    for s in range(1, groups):

        @pl.when(position + s >= groups)
        def _():
            for copy in turns[s - 1]:
                copy.start()

    def up(s):
        @pl.when(position + s < groups)
        def _():
            pl.semaphore_wait(ready.at[s], 1)
            for copy in (tails if s == 1 else []) + turns[s - 1]:
                copy.start()

    ext[:, :START, :] = jnp.zeros((blocks + 2, START, BLK), f32)
    for c in range(1, blocks + 1):
        spread(ext, pair_data, four_data, c, HEAD, steps)
        shape[c] = mark[c - 1]
        turned[c] = turn(shape[c])
    fixed = [(n, n + 1) for n in range(blocks)] + [(0, 0), (blocks - 1, blocks + 1)]
    for p, (r, c) in enumerate(fixed[:blocks]):
        fill(main, fine, sample, p, turned[c], shape[r + 1])
        contract(pair_data, four_data, main, fine, wide, narrow, p, c, HEAD, rows)
        if p == 0:
            up(1)

    for copy in marks:
        copy.wait()
    for c in (0, blocks + 1):
        turned[c] = turn(shape[c])
    order = list(fixed)
    order += [(list_ref[0, p], list_ref[1, p]) for p in range(len(fixed), pairs)]
    for p in range(blocks, pairs):
        r, c = order[p]
        fill(main, fine, sample, p, turned[c], shape[r + 1])

    for copy in edges:
        copy.wait()
    for n, c in enumerate((0, blocks + 1)):
        spread(ext, pair_data, four_data, c, HEAD, steps)
        contract(pair_data, four_data, main, fine, wide, narrow, blocks + n, c, HEAD, rows)
    for p in range(len(fixed), pairs - 1):
        contract(pair_data, four_data, main, fine, wide, narrow, p, order[p][1], HEAD, rows)
    for s in range(2, groups):
        up(s)

    def collect(first, last):
        for r in range(blocks):
            total = None
            for p, (row, _) in enumerate(fixed):
                if row == r:
                    term = gather(wide, narrow, p, first, last)
                    total = term if total is None else total + term
            out_ref[first:last, r * BLK : (r + 1) * BLK] = total
        for p in range(len(fixed), pairs):
            total = gather(wide, narrow, p, first, last)
            for r in range(blocks):
                lanes = slice(r * BLK, (r + 1) * BLK)
                out_ref[first:last, lanes] = out_ref[first:last, lanes] + jnp.where(
                    targets[p] == r, total, 0.0
                )

    targets = {
        p: jnp.where(p < count_ref[0], order[p][0], blocks) for p in range(len(fixed), pairs)
    }
    around = jnp.where(position == 0, math.exp(NT * math.log(damping)), 1.0)
    local = lax.broadcasted_iota(jnp.int32, (steps, BLK), 0)
    growth = jnp.exp((position * steps + local).astype(f32) * -math.log(damping)) / (NT * SCALE)
    growth = jnp.where(local % 2 == 0, -growth, growth)
    pick = lax.broadcasted_iota(jnp.int32, (2 * GEO, BLK), 0)

    def follow(c, before):
        ext[c, START - TAIL : START, :] = before * around
        spread(ext, pair_data, four_data, c, 0, HEAD + LEAD)

    for copy in tails:
        copy.wait()
    for c in range(1, blocks + 1):
        follow(c, head[:, (c - 1) * BLK : c * BLK])
    follow(0, corner[0])
    follow(blocks + 1, corner[1])
    for p in range(blocks):
        contract(pair_data, four_data, main, fine, wide, narrow, p, p + 1, 0, HEAD)
    contract(pair_data, four_data, main, fine, wide, narrow, blocks, 0, 0, HEAD)
    contract(pair_data, four_data, main, fine, wide, narrow, blocks + 1, blocks + 1, 0, HEAD)
    for p in range(len(fixed), pairs):
        contract(pair_data, four_data, main, fine, wide, narrow, p, order[p][1], 0, HEAD if p < pairs - 1 else rows)

    if steps > HEAD:
        collect(HEAD, steps)
    collect(0, HEAD)
    for some in [nears] + turns:
        for copy in some:
            copy.wait()
    for c in range(blocks + 2):
        n, b = (1, blocks - 1) if c == 0 else (2, 0) if c > blocks else (0, c - 1)
        total = parts[b : b + 1, :] if n == 0 else slots[0, n, b : b + 1, :]
        for s in range(1, groups):
            total = total + slots[s, n, b : b + 1, :]
        total = jnp.broadcast_to(total, (2 * GEO, BLK))
        hi, low = split(total)
        sums[c] = jnp.where(pick == 0, total, jnp.where(pick == 1, low, 0.0)).astype(bf16)

    ranks = []
    for p in range(pairs):
        both = product(sums[order[p][1]], sample[p])
        ranks.append(both[0:1, :BLK] + (both[1:2, :BLK] + both[0:1, BLK:]))
    for r in range(blocks):
        rank = jnp.zeros((1, BLK), f32)
        for p in range(pairs):
            if p < len(fixed):
                rank = rank + ranks[p] if fixed[p][0] == r else rank
            else:
                rank = rank + jnp.where(targets[p] == r, ranks[p], 0.0)
        lanes = slice(r * BLK, (r + 1) * BLK)
        out_ref[:, lanes] = out_ref[:, lanes] + growth * rank


def per_device(traces, centroids, near_list, pair_count):
    steps, width = traces.shape
    blocks = width // BLK
    pairs = near_list.shape[1]
    groups = lax.axis_size("freq")
    count = 6 + 3 * groups
    hbm = pl.BlockSpec(memory_space=pltpu.HBM)
    given = [pltpu.with_memory_space_constraint(v, pltpu.HBM) for v in (traces, centroids)]
    return pl.pallas_call(
        operator,
        out_shape=pltpu.VMEM((steps, width), f32),
        in_specs=[hbm] * 4,
        out_specs=pl.BlockSpec(memory_space=pltpu.VMEM),
        scratch_shapes=[
            pltpu.VMEM((blocks + 2, START + steps, BLK), f32),
            pltpu.VMEM((TAIL, width), f32),
            pltpu.VMEM((groups, 3, GEO, BLK), f32),
            pltpu.VMEM((blocks, GEO, BLK), f32),
            pltpu.VMEM((GEO, BLK), f32),
            pltpu.VMEM((2, TAIL, BLK), f32),
            pltpu.VMEM((blocks + 2, 2 * GEO, BLK), bf16),
            pltpu.VMEM((3, width), f32),
            pltpu.SMEM((2, pairs), jnp.int32),
            pltpu.SMEM((1,), jnp.int32),
            pltpu.VMEM((blocks + 2, HEAD + steps, WIDE), bf16),
            pltpu.VMEM((blocks + 2, HEAD + steps, 8 * BLK), fp8),
            pltpu.VMEM((pairs, HALF * BLK, WIDE), bf16),
            pltpu.VMEM((pairs, 2 * CORR * BLK, WIDE), fp8),
            pltpu.VMEM((pairs, BLK, WIDE), bf16),
            pltpu.VMEM((pairs, LEAD + steps, WIDE), f32),
            pltpu.VMEM((pairs, LEAD + steps, WIDE), f32),
            pltpu.VMEM((blocks + 2, BLK, BLK), f32),
            pltpu.VMEM((blocks + 2, GEO, BLK), f32),
            pltpu.SemaphoreType.DMA((count,)),
            pltpu.SemaphoreType.DMA((count,)),
            pltpu.SemaphoreType.DMA((blocks + 3,)),
            pltpu.SemaphoreType.REGULAR((groups,)),
        ],
        compiler_params=pltpu.CompilerParams(
            collective_id=0, has_side_effects=True, vmem_limit_bytes=60 * 1024 * 1024
        ),
    )(near_list[0].T, pair_count, *given)


def solution(mesh):
    in_specs = (
        P("freq", ("grp", "panel")),
        P(None, ("grp", "panel")),
        P(("grp", "panel"), None, None),
        P(("grp", "panel")),
    )
    out_specs = P("freq", ("grp", "panel"))
    return jax.shard_map(
        per_device, mesh=mesh, in_specs=in_specs, out_specs=out_specs, check_vma=False
    )
```
